32 devices in a mesh: dp: 8 (over z, x), tensor: 4 (over y, core).
Axes of the slice: x: 2, y: 2, z: 4, core: 2. Of those that a mesh axis runs over, the one named last changes fastest.
Arguments:
- segments: bfloat16 [32, 704, 512], P('dp'), may hold values from -6 to 6
- seg_start: int32 [32, 704], P('dp'), may hold values from 0 to 2048, as said below
- seg_count: int32 [32], P('dp'), may hold values from 300 to 704, as said below
- norm_gain: bfloat16 [512], P('dp'), may hold values from 0.25 to 1.75
- norm_shift: bfloat16 [512], P('dp'), may hold values from -3 to 3
- qkv_weight: bfloat16 [512, 3, 512], P('dp', None, 'tensor'), may hold values from -0.25 to 0.25
- out_weight: bfloat16 [512, 512], P(('tensor', 'dp')), may hold values from -1 to 1
- ffn_gain: bfloat16 [512], P('dp'), may hold values from 0.25 to 1.75
- ffn_shift: bfloat16 [512], P('dp'), may hold values from -3 to 3
- up_weight: bfloat16 [512, 2048], P('dp', 'tensor'), may hold values from -0.25 to 0.25
- up_bias: bfloat16 [2048], P(('tensor', 'dp')), may hold values from -3 to 3
- down_weight: bfloat16 [2048, 512], P(('tensor', 'dp')), may hold values from -0.125 to 0.125
- cotangent: bfloat16 [32, 704, 512], P('dp'), may hold values from -6 to 6
Outputs:
- block_out: bfloat16 [32, 704, 512], P('dp')
- segments_grad: float32 [32, 704, 512], P('dp')
- norm_gain_grad: float32 [512], P('dp')
- norm_shift_grad: float32 [512], P('dp')
- qkv_weight_grad: float32 [512, 3, 512], P('dp', None, 'tensor')
- out_weight_grad: float32 [512, 512], P(('tensor', 'dp'))
- ffn_gain_grad: float32 [512], P('dp')
- ffn_shift_grad: float32 [512], P('dp')
- up_weight_grad: float32 [512, 2048], P('dp', 'tensor')
- up_bias_grad: float32 [2048], P(('tensor', 'dp'))
- down_weight_grad: float32 [2048, 512], P(('tensor', 'dp'))
The draws below stay inside these ranges and needn't reach their ends.
Inputs may be any that keep to these rules, and one draw needn't show every extreme that they name: One sequence has exactly 704 live segments and one exactly 300; slots at and after seg_count are padding. `seg_start`: 0 in the first slot, strictly rising over a sequence's live segments and below 2048 there; 2048 in every padded slot.
All inputs are finite; a program needn't handle non-finite values.
Results may differ from the reference program's by a relative error of at most 0.014.
Values may be sent and summed in bfloat16 or wider, within the bound.
No kernel may reach another device: no remote copies, remote signals or barrier semaphores. Data moves between devices by JAX's collectives and lax.ppermute only.
A program may use at most 128 MiB of HBM per device.

```python
import math
import jax
import jax.numpy as jnp
from jax import lax

D = 512
HEADS = 8
HEAD = 64
FF = 2048
SEG = 704
SEG_MIN = 300
BYTES = 2048
SEQS = 32


def draw_counts_common(key):
    count_key = jax.random.fold_in(key, 11)
    counts = jax.random.randint(count_key, (SEQS,), SEG_MIN, SEG + 1, dtype=jnp.int32)
    return counts.at[0].set(SEG).at[1].set(SEG_MIN)


def draw_seg_count(key, part):
    return draw_counts_common(key)


def pick_bytes(seq_key):
    return jax.random.permutation(seq_key, BYTES - 1)[:SEG - 1].astype(jnp.int32) + 1


def draw_seg_start(key, part):
    counts = draw_counts_common(key)
    order_keys = jax.random.split(jax.random.fold_in(key, 23), SEQS)
    chosen = jax.vmap(pick_bytes)(order_keys)
    places = jnp.arange(SEG - 1, dtype=jnp.int32)
    marked = jnp.where(places[None, :] < counts[:, None] - 1, chosen, BYTES)
    ordered = jnp.sort(marked, axis=1)
    return jnp.concatenate([jnp.zeros((SEQS, 1), jnp.int32), ordered.astype(jnp.int32)], axis=1)


def raised(entries, key, source, target, parts, factor):
    owner, partner = [(jnp.arange(entries.shape[position]) // (entries.shape[position] // parts)).reshape([-1 if axis == position else 1 for axis in range(entries.ndim)]) for position in (source, target)]
    chosen = jax.random.permutation(key, parts)[partner]
    strong = (owner == chosen) | (owner == (partner + parts // 2) % parts)
    return jnp.where(strong, factor * entries, entries)


def block_levels(own_key, shape, shards, smallest, top_value):
    def one(dim, parts):
        steps = jax.random.uniform(jax.random.fold_in(jax.random.fold_in(own_key, 6), dim), (parts,), jnp.float32, smallest / len(shards), top_value / len(shards))
        return jnp.repeat(jnp.exp(steps), shape[dim] // parts).reshape((-1,) + (1,) * (len(shape) - dim - 1))

    gain = one(*shards[0])
    for cut in shards[1:]:
        gain = gain * one(*cut)
    return gain


def noise(stream_key, dims, scale, bound, cuts=(), held_as=jnp.bfloat16):
    entries = scale * jax.random.normal(stream_key, dims, jnp.float32)
    if cuts:
        entries = entries * block_levels(stream_key, dims, cuts, -0.22, 0.18)
    return jnp.clip(entries, -bound, bound).astype(held_as)


def gaussian_with(stream_key, dims, scale, reach, cuts, heavy, kind=jnp.bfloat16):
    values = scale * jax.random.normal(stream_key, dims, jnp.float32)
    if cuts:
        values = values * block_levels(stream_key, dims, cuts, -0.22, 0.18)
    return jnp.clip(raised(values, jax.random.fold_in(stream_key, 3), *heavy), -reach, reach).astype(kind)


def setup_inputs(seed: int = 0) -> dict:
    key_of = jax.random.split(jax.random.key(seed), 14)
    return {
        "segments": gaussian_with(key_of[0], (SEQS, SEG, D), 1.0, 6.0, ((0, 8),), (0, 2, 8, 2.0)),
        "seg_start": draw_seg_start(jax.random.fold_in(key_of[13], 71), 0),
        "seg_count": draw_seg_count(jax.random.fold_in(key_of[13], 71), 0),
        "norm_gain": jnp.clip(1.0 + 0.15 * jax.random.normal(key_of[3], (D,), jnp.float32), 0.25, 1.75).astype(jnp.bfloat16),
        "norm_shift": noise(key_of[4], (D,), 0.5, 3.0, ((0, 8),)),
        "qkv_weight": noise(key_of[5], (D, 3, D), D ** -0.5, 0.25, ((0, 8), (2, 4))),
        "out_weight": noise(key_of[6], (D, D), (D // 16) ** -0.5, 1.0, ((0, 32),)),
        "ffn_gain": jnp.clip(1.0 + 0.15 * jax.random.normal(key_of[7], (D,), jnp.float32), 0.25, 1.75).astype(jnp.bfloat16),
        "ffn_shift": noise(key_of[8], (D,), 0.5, 3.0, ((0, 8),)),
        "up_weight": noise(key_of[9], (D, FF), D ** -0.5, 0.25, ((0, 8), (1, 4))),
        "up_bias": noise(key_of[10], (FF,), 0.5, 3.0, ((0, 32),)),
        "down_weight": noise(key_of[11], (FF, D), FF ** -0.5, 0.125, ((0, 32),)),
        "cotangent": noise(key_of[12], (SEQS, SEG, D), 1.0, 6.0, ((0, 8),)),
    }


EPSILON = 1e-05
MASKED = -1e+30
HIGHEST = lax.Precision.HIGHEST

@jax.custom_vjp
def low(v):
    return lax.optimization_barrier(v.astype(jnp.bfloat16)).astype(jnp.float32)

@jax.custom_vjp
def low_back(v):
    return v

def low_keep(v):
    return (low(v), None)

def low_pass(kept, grad):
    return (grad,)

def back_keep(v):
    return (v, None)

def back_low(kept, grad):
    return (low(grad),)
low.defvjp(low_keep, low_pass)
low_back.defvjp(back_keep, back_low)

def normalize(values, scale_vec, offset_vec):
    centre = lax.optimization_barrier(jnp.mean(values, axis=-1, keepdims=True))
    centred = values - centre
    spread = lax.optimization_barrier(jnp.mean(centred * centred, axis=-1, keepdims=True))
    return centred * lax.rsqrt(spread + EPSILON) * scale_vec + offset_vec

def rotate(values, cosine, sine_term):
    half_size = values.shape[-1] // 2
    turned = jnp.concatenate([-values[..., half_size:], values[..., :half_size]], axis=-1)
    return values * cosine + turned * sine_term

def rotary_tables(starts, head_size):
    half_size = head_size // 2
    freq_index = jnp.arange(half_size).astype(jnp.float32)
    inverse = jnp.exp(freq_index * (-math.log(10000.0) / half_size))
    angles = starts.astype(jnp.float32)[..., None] * inverse
    angles = jnp.concatenate([angles, angles], axis=-1)
    return (jnp.cos(angles), jnp.sin(angles))

def allowed_keys(length, live_count):
    places = jnp.arange(length)
    return (places[None, :] <= places[:, None]) & (places[None, :] < live_count)

def attend(packed):
    queries, key_rows, value_rows, live_count = packed
    scores = low_back(jnp.einsum('qhd,khd->hqk', queries, key_rows, precision=HIGHEST))
    allowed = allowed_keys(queries.shape[0], live_count)
    scores = jnp.where(allowed[None], scores, MASKED)
    attention_probs = jax.nn.softmax(scores, axis=-1)
    return jnp.einsum('hqk,khd->qhd', low(attention_probs), value_rows, precision=HIGHEST)

def reference(segments, seg_start, seg_count, norm_gain, norm_shift, qkv_weight, out_weight, ffn_gain, ffn_shift, up_weight, up_bias, down_weight, cotangent):
    cosine, sine_term = rotary_tables(seg_start, HEAD)
    cosine = cosine[:, :, None, :]
    sine_term = sine_term[:, :, None, :]

    def forward(inputs, gain_one, shift_one, w_qkv, w_out, gain_two, shift_two, w_up, b_up, w_down):
        attn_in = low(normalize(inputs, gain_one, shift_one))
        projected = low_back(jnp.einsum('snd,dct->snct', attn_in, w_qkv, precision=HIGHEST))
        shaped = projected.reshape(SEQS, SEG, 3, HEADS, HEAD)
        queries = low(rotate(shaped[:, :, 0], cosine, sine_term) * HEAD ** (-0.5))
        key_rows = low(rotate(shaped[:, :, 1], cosine, sine_term))
        value_rows = low(shaped[:, :, 2])
        mixed_rows = lax.map(jax.checkpoint(attend), (queries, key_rows, value_rows, seg_count))
        mixed_rows = low_back(low(mixed_rows)).reshape(SEQS, SEG, D)
        attn_full = low_back(jnp.einsum('snt,td->snd', mixed_rows, w_out, precision=HIGHEST))
        residual = inputs + attn_full
        ffn_in = low(normalize(residual, gain_two, shift_two))
        pre_act = low_back(jnp.einsum('snd,df->snf', ffn_in, w_up, precision=HIGHEST) + b_up)
        act_low = low(jax.nn.gelu(pre_act, approximate=False))
        return residual + jnp.einsum('snf,fd->snd', act_low, w_down, precision=HIGHEST)
    primal = (segments.astype(jnp.float32), norm_gain.astype(jnp.float32), norm_shift.astype(jnp.float32), qkv_weight.astype(jnp.float32), out_weight.astype(jnp.float32), ffn_gain.astype(jnp.float32), ffn_shift.astype(jnp.float32), up_weight.astype(jnp.float32), up_bias.astype(jnp.float32), down_weight.astype(jnp.float32))
    output, pullback = jax.vjp(forward, *primal)
    gradients = pullback(cotangent.astype(jnp.float32))
    return (output.astype(jnp.bfloat16), gradients[0], gradients[1], gradients[2], gradients[3], gradients[4], gradients[5], gradients[6], gradients[7], gradients[8], gradients[9])
```

```python
import math

import jax
import jax.numpy as jnp
from jax import lax
from jax.experimental import pallas as pl
from jax.experimental.pallas import tpu as pltpu
from jax.sharding import PartitionSpec as P

HEAD = 64
PAIR = 2 * HEAD
BLOCK = 256
EPSILON = 1e-05
MASKED = -1e30
BF16 = jnp.bfloat16
F32 = jnp.float32
EXTRA = 16


def nn(a, b):
    return lax.dot_general(a, b, (((1,), (0,)), ((), ())), preferred_element_type=F32)


def nt(a, b):
    return lax.dot_general(a, b, (((1,), (1,)), ((), ())), preferred_element_type=F32)


def call(kernel, operands, outs, scratch=(), scalars=0, name=None):
    inner = [pl.BlockSpec(memory_space=pltpu.SMEM) for _ in range(scalars)]
    inner += [pl.BlockSpec(memory_space=pltpu.VMEM) for _ in operands[scalars:]]
    return pl.pallas_call(
        kernel,
        in_specs=inner,
        out_specs=[pl.BlockSpec(memory_space=pltpu.VMEM) for _ in outs],
        out_shape=[jax.ShapeDtypeStruct(s, d) for s, d in outs],
        scratch_shapes=list(scratch),
        compiler_params=pltpu.CompilerParams(vmem_limit_bytes=40 * 1024 * 1024),
        name=name,
    )(*operands)


def digits(size):
    out = []
    while size > 1:
        radix = math.gcd(size, 8)
        radix = size if radix == 1 else radix
        out.insert(0, radix)
        size //= radix
    return out or [1]


def step_list(radices):
    steps = [()]
    for radix in radices:
        steps = [s + (k,) for s in steps for k in range(radix)]
    return steps


def moved(index, radices, steps):
    target, scale = 0, 1
    for radix, step in zip(reversed(radices), reversed(steps)):
        target = target + (index % radix + step + radix) % radix * scale
        index = index // radix
        scale *= radix
    return target


def sent_ahead(value, radices, steps):
    size = math.prod(radices)
    return lax.ppermute(value, "dp", [(i, moved(i, radices, steps)) for i in range(size)])


def one_step(radices, place, k):
    return tuple(k if p == place else 0 for p in range(len(radices)))


def gather_pieces(piece, radices):
    held = {(): piece}
    for place, radix in enumerate(radices):
        held = {
            key + (k,): sent_ahead(value, radices, one_step(radices, place, k)) if k else value
            for key, value in held.items()
            for k in range(radix)
        }
    return [held[s] for s in step_list(radices)]


def scatter_pieces(pieces, radices):
    held = dict(zip(step_list(radices), pieces))
    for place in range(len(radices)):
        arrived = {}
        for key, value in held.items():
            steps = one_step(radices, place, key[0])
            got = sent_ahead(value, radices, steps) if key[0] else value
            arrived.setdefault(key[1:], []).append(got)
        last = place + 1 == len(radices)
        held = {
            key: (sum(v.astype(F32) for v in values) if last else
                  sum(v.astype(F32) for v in values).astype(values[0].dtype))
            for key, values in arrived.items()
        }
    return held[()]


def swap(value, bit):
    return lax.ppermute(value, "tensor", [(t, t ^ bit) for t in range(lax.axis_size("tensor"))])


def behind(radices):
    here = lax.axis_index("dp")
    return [moved(here, radices, tuple(-k for k in s)) for s in step_list(radices)]


def ahead(radices):
    here = lax.axis_index("dp")
    return [moved(here, radices, s) for s in step_list(radices)]


def in_place(pieces, order, parts):
    if all(rows % 16 == 0 for rows in parts):
        return pieces, order, parts
    count = len(pieces)
    stacked = jnp.stack(pieces)
    where = jnp.zeros((count,), jnp.int32).at[order].set(jnp.arange(count, dtype=jnp.int32))
    stacked = stacked[where]
    laid, at = [], 0
    for rows in parts:
        laid.append(stacked[:, at : at + rows].reshape(count * rows, -1))
        at += rows
    if at < stacked.shape[1]:
        laid.append(stacked[:, at:].astype(F32).sum(axis=0).astype(stacked.dtype))
    return [jnp.concatenate(laid)], jnp.zeros((1,), jnp.int32), [count * r for r in parts]


def norm_parts(rows):
    centred = rows - jnp.mean(rows, axis=-1, keepdims=True)
    rstd = lax.rsqrt(jnp.mean(centred * centred, axis=-1, keepdims=True) + EPSILON)
    return centred * rstd, rstd


def norm_pull(grad, gain, xhat, rstd):
    scaled = grad * gain
    level = jnp.mean(scaled, axis=-1, keepdims=True)
    along = jnp.mean(scaled * xhat, axis=-1, keepdims=True)
    return rstd * (scaled - level - xhat * along)


def colsum(rows):
    return jnp.sum(rows, axis=0, keepdims=True)


def enter(seg, pieces, order, rows, seg_len, padded, width, cols):
    count = len(pieces)

    def kernel(order_ref, seg_ref, *refs):
        parts = refs[:count]
        w_out, xt_out, vec_out, x_scr = refs[count:]
        for k in range(count):
            start = pl.multiple_of(order_ref[k] * rows, 16)
            w_out[pl.ds(start, rows), :] = parts[k][0:rows, :]
        vec = parts[0][rows:, :].astype(F32)
        for k in range(1, count):
            vec = vec + parts[k][rows:, :].astype(F32)
        vec_out[...] = jnp.zeros(vec_out.shape, F32)
        for v in range(5):
            vec_out[v : v + 1, 0:cols] = vec[2 * v : 2 * v + 1, :]
            vec_out[v : v + 1, cols:width] = vec[2 * v + 1 : 2 * v + 2, 0 : width - cols]
        gain = vec_out[0:1, :]
        shift = vec_out[1:2, :]
        step = seg_len // 4

        def body(c, carry):
            at = pl.multiple_of(c * step, 16)
            xhat, _ = norm_parts(seg_ref[pl.ds(at, step), :].astype(F32))
            x_scr[pl.ds(at, step), :] = (xhat * gain + shift).astype(BF16)
            return carry

        lax.fori_loop(0, 4, body, 0)
        x_scr[seg_len:padded, :] = jnp.zeros((padded - seg_len, width), BF16)
        xt_out[...] = x_scr[...].T

    return call(
        kernel,
        (order, seg, *pieces),
        [((width, cols), BF16), ((width, padded), BF16), ((8, width), F32)],
        [pltpu.VMEM((padded, width), BF16)],
        scalars=1,
        name="enter",
    )


def lay_out(pieces, order, parts, vec, width):
    count = len(pieces)
    out_rows, up_rows, down_rows = parts

    def kernel(order_ref, vec_ref, *refs):
        got = refs[:count]
        out_ref, ud_ref = refs[count:]
        up_all = count * up_rows
        down_all = count * down_rows
        for k in range(count):
            o = order_ref[k]
            piece = got[k]
            a, b = out_rows, out_rows + up_rows
            out_ref[pl.ds(pl.multiple_of(o * out_rows, 16), out_rows), :] = piece[0:a, :]
            ud_ref[pl.ds(pl.multiple_of(o * up_rows, 16), up_rows), :] = piece[a:b, :]
            ud_ref[pl.ds(pl.multiple_of(up_all + o * down_rows, 16), down_rows), :] = piece[b:, :]
        ud_ref[up_all + down_all :, :] = jnp.broadcast_to(vec_ref[4:5, :], (EXTRA, width)).astype(BF16)

    return call(
        kernel,
        (order, vec, *pieces),
        [
            ((count * out_rows, width), BF16),
            ((count * (up_rows + down_rows) + EXTRA, width), BF16),
        ],
        scalars=1,
        name="lay_out",
    )


def blocks_of(seg_len):
    return [(s, min(s + BLOCK, seg_len)) for s in range(0, seg_len, BLOCK)]


def one_head(block, h):
    zero = jnp.zeros_like(block)
    return jnp.concatenate([block, zero] if h == 0 else [zero, block], axis=0)


def allowed_slots(live, start, stop):
    place = lax.broadcasted_iota(jnp.int32, (1, BLOCK), 1) + start
    bound = jnp.minimum(place, live - 1)
    return lax.broadcasted_iota(jnp.int32, (stop, BLOCK), 0) <= bound


def attend_forward(live, xt, w, cos, sin, seg_len):
    width, padded = xt.shape
    half = HEAD // 2

    def kernel(live_ref, xt_ref, w_ref, cos_ref, sin_ref, qkv_out, ot_out, mixed_out, lse_out):
        proj = nn(w_ref[0:width, :].T, xt_ref[...])
        cosine = cos_ref[...]
        sine = sin_ref[...]

        def rot(z):
            a, b = z[0:half], z[half:]
            return jnp.concatenate([a * cosine - b * sine, b * cosine + a * sine], axis=0)

        for h in range(2):
            r = h * HEAD
            qkv_out[r : r + HEAD, :] = (rot(proj[r : r + HEAD]) * HEAD ** (-0.5)).astype(BF16)
            r = r + PAIR
            qkv_out[r : r + HEAD, :] = rot(proj[r : r + HEAD]).astype(BF16)
        qkv_out[2 * PAIR :, :] = proj[2 * PAIR :].astype(BF16)
        keys = qkv_out[PAIR : 2 * PAIR, :].T
        lse_out[...] = jnp.zeros(lse_out.shape, F32)
        for start, stop in blocks_of(seg_len):
            cols = slice(start, start + BLOCK)
            allowed = allowed_slots(live_ref[0], start, stop)
            for h in range(2):
                r = h * HEAD
                query = one_head(qkv_out[r : r + HEAD, cols], h)
                scores = jnp.where(allowed, nn(keys[0:stop], query), MASKED)
                top = jnp.max(scores, axis=0, keepdims=True)
                weights = jnp.exp(scores - top)
                total = colsum(weights)
                probs = (weights * (1.0 / total)).astype(BF16)
                value = qkv_out[2 * PAIR + r : 2 * PAIR + r + HEAD, 0:stop]
                ot_out[r : r + HEAD, cols] = nn(value, probs).astype(BF16)
                lse_out[h : h + 1, cols] = top + jnp.log(total)
        mixed_out[...] = ot_out[...].T[0:seg_len]

    return call(
        kernel,
        (live, xt, w, cos, sin),
        [
            ((3 * PAIR, padded), BF16),
            ((PAIR, padded), BF16),
            ((seg_len, PAIR), BF16),
            ((8, padded), F32),
        ],
        scalars=1,
        name="attend_forward",
    )


def emit(whole, pieces, order_ref, spans):
    for k, piece in enumerate(pieces):
        at = 0
        for first, rows in spans:
            start = pl.multiple_of(first + order_ref[k] * rows, 16)
            piece[at : at + rows, :] = whole[pl.ds(start, rows), :]
            at += rows


def attend_backward(live, xt, w, cos, sin, qkv, ot, lse, dot, acc, seg_len):
    width, padded = xt.shape
    half = HEAD // 2
    n_acc = len(acc)

    def kernel(live_ref, xt_ref, w_ref, cos_ref, sin_ref, qkv_ref, ot_ref, lse_ref, dot_ref, *refs):
        acc_refs = refs[:n_acc]
        acc_out, grad_out, d_scr, pg_scr = refs[n_acc:]
        cosine = cos_ref[...]
        sine = sin_ref[...]
        keys = qkv_ref[PAIR : 2 * PAIR, :].T
        values = qkv_ref[2 * PAIR :, :].T
        prod = dot_ref[...].astype(F32) * ot_ref[...].astype(F32)
        inner = [colsum(prod[h * HEAD : h * HEAD + HEAD]) for h in range(2)]
        d_scr[...] = jnp.zeros(d_scr.shape, F32)
        for start, stop in blocks_of(seg_len):
            cols = slice(start, start + BLOCK)
            allowed = allowed_slots(live_ref[0], start, stop)
            for h in range(2):
                r = h * HEAD
                k = PAIR + r
                v = 2 * PAIR + r
                query = qkv_ref[r : r + HEAD, cols]
                out_grad = dot_ref[r : r + HEAD, cols]
                scores = jnp.where(allowed, nn(keys[0:stop], one_head(query, h)), MASKED)
                probs = jnp.exp(scores - lse_ref[h : h + 1, cols])
                prob_grad = nn(values[0:stop], one_head(out_grad, h))
                score_grad = (probs * (prob_grad - inner[h][:, cols])).astype(BF16)
                d_scr[r : r + HEAD, cols] = nn(qkv_ref[k : k + HEAD, 0:stop], score_grad)
                d_scr[k : k + HEAD, 0:stop] += nt(query, score_grad)
                d_scr[v : v + HEAD, 0:stop] += nt(out_grad, probs.astype(BF16))

        def unrot(z):
            a, b = z[0:half], z[half:]
            return jnp.concatenate([a * cosine + b * sine, b * cosine - a * sine], axis=0)

        for h in range(2):
            r = h * HEAD
            pg_scr[r : r + HEAD, :] = (unrot(d_scr[r : r + HEAD, :]) * HEAD ** (-0.5)).astype(BF16)
            r = r + PAIR
            pg_scr[r : r + HEAD, :] = unrot(d_scr[r : r + HEAD, :]).astype(BF16)
        pg_scr[2 * PAIR :, :] = d_scr[2 * PAIR :, :].astype(BF16)
        part = nn(w_ref[0:width, :], pg_scr[...])
        acc_out[...] = acc_refs[0][...] + part if n_acc else part
        grad_out[...] = nt(xt_ref[...], pg_scr[...]).astype(BF16)

    return call(
        kernel,
        (live, xt, w, cos, sin, qkv, ot, lse, dot, *acc),
        [((width, padded), F32), ((width, 3 * PAIR), BF16)],
        [pltpu.VMEM((3 * PAIR, padded), F32), pltpu.VMEM((3 * PAIR, padded), BF16)],
        scalars=1,
        name="attend_backward",
    )


def combine(parts, order, spans, count, keep):
    rows, cols = parts[0].shape
    tail = rows - keep
    piece_rows = sum(r for _, r in spans) + tail

    def kernel(order_ref, *refs):
        got = refs[: len(parts)]
        pieces = refs[len(parts) : -1]
        whole = refs[-1]
        total = got[0][...].astype(F32)
        for p in got[1:]:
            total = total + p[...].astype(F32)
        whole[...] = total.astype(BF16)
        emit(whole, pieces, order_ref, spans)
        if tail:
            for piece in pieces:
                piece[piece_rows - tail :, :] = whole[keep:, :]

    return call(
        kernel,
        (order, *parts),
        [((piece_rows, cols), BF16)] * count,
        [pltpu.VMEM((rows, cols), BF16)],
        scalars=1,
        name="combine",
    )


def merge_attention(seg, mixed, outs, vec):
    rows, width = seg.shape
    n = len(mixed)

    def kernel(seg_ref, vec_ref, *refs):
        mixed_refs, out_refs = refs[:n], refs[n : 2 * n]
        res_out, ffn_out = refs[2 * n :]
        gain = vec_ref[2:3, :]
        shift = vec_ref[3:4, :]
        step = rows // 2

        def body(c, carry):
            at = pl.multiple_of(c * step, 16)
            here = pl.ds(at, step)
            total = nn(mixed_refs[0][here, :], out_refs[0][...])
            for r in range(1, n):
                total = total + nn(mixed_refs[r][here, :], out_refs[r][...])
            total = total + seg_ref[here, :].astype(F32)
            res_out[here, :] = total
            xhat, _ = norm_parts(total)
            ffn_out[here, :] = (xhat * gain + shift).astype(BF16)
            return carry

        lax.fori_loop(0, 2, body, 0)

    return call(
        kernel,
        (seg, vec, *mixed, *outs),
        [((rows, width), F32), ((rows, width), BF16)],
        name="merge_attention",
    )


def feed_forward(ffn_in, cot, ud, acc):
    rows, width = ffn_in.shape
    units = (ud.shape[0] - EXTRA) // 2
    n_acc = len(acc)

    def kernel(x_ref, cot_ref, ud_ref, *refs):
        acc_refs = refs[:n_acc]
        out_acc, back_acc, grad_out, act_scr, pg_scr = refs[n_acc:]
        step = rows // 2
        bias = ud_ref[2 * units : 2 * units + 1, :].astype(F32)

        def body(c, total):
            at = pl.multiple_of(c * step, 16)
            here = pl.ds(at, step)
            up = ud_ref[0:units, :]
            down = ud_ref[units : 2 * units, :]
            pre = nn(x_ref[here, :], up) + bias
            below = 0.5 + 0.5 * lax.erf(pre * 0.5**0.5)
            act = (pre * below).astype(BF16)
            slope = below + pre * (jnp.exp(-0.5 * (pre * pre)) * (1.0 / math.sqrt(2.0 * math.pi)))
            pre_grad = (nt(cot_ref[here, :], down) * slope).astype(BF16)
            act_scr[here, :] = act
            pg_scr[here, :] = pre_grad
            fwd = nn(act, down)
            back = nt(pre_grad, up)
            if n_acc:
                fwd = fwd + acc_refs[0][here, :]
                back = back + acc_refs[1][here, :]
            out_acc[here, :] = fwd
            back_acc[here, :] = back
            return total + colsum(pre_grad.astype(F32))

        total = lax.fori_loop(0, 2, body, jnp.zeros((1, units), F32))
        grad_out[0:units, :] = nn(x_ref[...].T, pg_scr[...]).astype(BF16)
        grad_out[units : 2 * units, :] = nn(act_scr[...].T, cot_ref[...]).astype(BF16)
        grad_out[2 * units :, :] = jnp.broadcast_to(total, (EXTRA, units)).astype(BF16)

    return call(
        kernel,
        (ffn_in, cot, ud, *acc),
        [((rows, width), F32), ((rows, width), F32), ((2 * units + EXTRA, width), BF16)],
        [pltpu.VMEM((rows, units), BF16), pltpu.VMEM((rows, units), BF16)],
        name="feed_forward",
    )


def turn_back(res, forward, backward, cot, vec, mixed_t, outs, padded):
    rows, width = res.shape
    n = len(outs)

    def kernel(res_ref, fwd_ref, back_ref, cot_ref, vec_ref, *refs):
        mixed_refs, out_refs = refs[:n], refs[n : 2 * n]
        block_out, resid_out, vec_out = refs[2 * n : 2 * n + 3]
        grad_outs = refs[2 * n + 3 : 3 * n + 3]
        dot_outs = refs[3 * n + 3 : 4 * n + 3]
        low_scr = refs[-1]
        gain = vec_ref[2:3, :]
        step = rows // 4

        def body(c, sums):
            here = pl.ds(pl.multiple_of(c * step, 16), step)
            res_rows = res_ref[here, :]
            back = back_ref[here, :]
            block_out[here, :] = (res_rows + fwd_ref[here, :]).astype(BF16)
            xhat, rstd = norm_parts(res_rows)
            resid = cot_ref[here, :].astype(F32) + norm_pull(back, gain, xhat, rstd)
            resid_out[here, :] = resid
            low_scr[here, :] = resid.astype(BF16)
            return sums[0] + colsum(back * xhat), sums[1] + colsum(back)

        zero = jnp.zeros((1, width), F32)
        gain_grad, shift_grad = lax.fori_loop(0, 4, body, (zero, zero))
        vec_out[...] = jnp.zeros(vec_out.shape, F32)
        vec_out[0:1, :] = gain_grad
        vec_out[1:2, :] = shift_grad
        low_scr[rows:, :] = jnp.zeros((padded - rows, width), BF16)
        for r in range(n):
            dot_outs[r][...] = nt(out_refs[r][...], low_scr[...]).astype(BF16)
            grad_outs[r][...] = nn(mixed_refs[r][...], low_scr[...]).astype(BF16)

    return call(
        kernel,
        (res, forward, backward, cot, vec, *mixed_t, *outs),
        [((rows, width), BF16), ((rows, width), F32), ((8, width), F32)]
        + [((PAIR, width), BF16)] * n
        + [((PAIR, padded), BF16)] * n,
        [pltpu.VMEM((padded, width), BF16)],
        name="turn_back",
    )


def leave(seg, resid, acc, vec):
    rows, width = seg.shape
    padded = acc.shape[1]

    def kernel(seg_ref, resid_ref, acc_ref, vec_ref, seg_out, vec_out, acc_scr):
        gain = vec_ref[0:1, :]
        step = rows // 4
        acc_scr[...] = acc_ref[...].T

        def body(c, sums):
            here = pl.ds(pl.multiple_of(c * step, 16), step)
            grad = acc_scr[here, :]
            xhat, rstd = norm_parts(seg_ref[here, :].astype(F32))
            seg_out[here, :] = (resid_ref[here, :] + norm_pull(grad, gain, xhat, rstd)).astype(BF16)
            return sums[0] + colsum(grad * xhat), sums[1] + colsum(grad)

        zero = jnp.zeros((1, width), F32)
        gain_grad, shift_grad = lax.fori_loop(0, 4, body, (zero, zero))
        vec_out[...] = jnp.zeros(vec_out.shape, F32)
        vec_out[0:1, :] = gain_grad
        vec_out[1:2, :] = shift_grad

    return call(
        kernel,
        (seg, resid, acc, vec),
        [((rows, width), BF16), ((8, width), F32)],
        [pltpu.VMEM((padded, width), F32)],
        name="leave",
    )


def spread(mine, tensor_index, dtype):
    other = swap(mine, 2)
    near = swap(mine, 1)
    far = swap(other, 1)
    got = [mine, near, other, far]
    odd = (tensor_index & 1) == 1
    high = (tensor_index & 2) == 2
    low = [jnp.where(odd, got[1], got[0]), jnp.where(odd, got[0], got[1])]
    top = [jnp.where(odd, got[3], got[2]), jnp.where(odd, got[2], got[3])]
    out = [jnp.where(high, top[a], low[a]) for a in range(2)]
    out += [jnp.where(high, low[a], top[a]) for a in range(2)]
    return jnp.stack(out).astype(dtype)


def rotary_tables(starts, padded):
    half = HEAD // 2
    inverse = jnp.exp(jnp.arange(half).astype(F32) * (-math.log(10000.0) / half))
    angles = inverse[:, None] * starts.astype(F32)[None, :]
    angles = jnp.pad(angles, ((0, 0), (0, padded - starts.shape[0])))
    return jnp.cos(angles), jnp.sin(angles)


def vector_rows(vectors, here, width, cols):
    rows = []
    for v in vectors:
        full = jnp.zeros((width,), BF16)
        full = lax.dynamic_update_slice(full, v, (here * v.shape[0],))
        rows.append(jnp.pad(full, (0, 2 * cols - width)).reshape(2, cols))
    rows.append(jnp.zeros((EXTRA - 2 * len(vectors), cols), BF16))
    return jnp.concatenate(rows)


def cut(total, here, spans_rows):
    out, at = [], 0
    for rows in spans_rows:
        out.append(total[at : at + rows])
        at += rows
    return out


def local(
    segments,
    seg_start,
    seg_count,
    norm_gain,
    norm_shift,
    qkv_weight,
    out_weight,
    ffn_gain,
    ffn_shift,
    up_weight,
    up_bias,
    down_weight,
    cotangent,
):
    seq_local, seg_len, width = segments.shape
    tensor = lax.axis_size("tensor")
    members = lax.axis_size("dp")
    assert seq_local == tensor == 4
    padded = -(-seg_len // BLOCK) * BLOCK
    radices = digits(members)
    here = lax.axis_index("dp")
    mine = lax.axis_index("tensor")
    cols = 3 * qkv_weight.shape[2]
    assert cols == 3 * PAIR and width * 2 > cols
    groups = range(tensor)

    seg = lax.dynamic_index_in_dim(segments, mine, 0, keepdims=False)
    cot = lax.dynamic_index_in_dim(cotangent, mine, 0, keepdims=False)
    starts = lax.dynamic_index_in_dim(seg_start, mine, 0, keepdims=False)
    live = lax.dynamic_slice_in_dim(seg_count, mine, 1)
    cos, sin = rotary_tables(starts, padded)
    back_order = jnp.stack(behind(radices)).astype(jnp.int32)
    ahead_order = jnp.stack(ahead(radices)).astype(jnp.int32)

    vectors = (norm_gain, norm_shift, ffn_gain, ffn_shift, up_bias)
    first = jnp.concatenate(
        [qkv_weight.reshape(-1, cols), vector_rows(vectors, here, width, cols)]
    )
    second = jnp.concatenate([out_weight, up_weight, down_weight])
    second_parts = (out_weight.shape[0], up_weight.shape[0], down_weight.shape[0])
    got = gather_pieces(first, radices)
    pieces, order, parts = in_place(got, back_order, (qkv_weight.shape[0],))
    w0, xt, vec = enter(seg, pieces, order, parts[0], seg_len, padded, width, cols)
    second, w0 = lax.optimization_barrier((second, w0))
    w = [w0, swap(w0, 1), swap(w0, 2), None]
    w[3] = swap(w[2], 1)
    got = gather_pieces(second, radices)
    pieces, order, parts = in_place(got, back_order, second_parts)
    o0, ud0 = lay_out(pieces, order, parts, vec, width)
    outs = [o0, swap(o0, 1), swap(o0, 2), None]
    outs[3] = swap(outs[2], 1)
    uds = [ud0, swap(ud0, 1), swap(ud0, 2), None]
    uds[3] = swap(uds[2], 1)

    heads = [attend_forward(live, xt, w[r], cos, sin, seg_len) for r in groups]
    res, ffn_in = merge_attention(seg, [h[2] for h in heads], outs, vec)
    acc = ()
    ffn_grads = [None] * 4
    for r in (3, 2, 1, 0):
        out_acc, back_acc, ffn_grads[r] = feed_forward(ffn_in, cot, uds[r], acc)
        acc = (out_acc, back_acc)
    turned = turn_back(res, *acc, cot, vec, [h[1] for h in heads], outs, padded)
    block_mine, resid, ffn_vec = turned[0:3]
    out_grads = turned[3:7]
    dots = turned[7:11]
    block_out = spread(block_mine, mine, BF16)

    def reduced(grads, parts_rows, keep):
        sums = [grads[0], swap(grads[1], 1)]
        two = (grads[2].astype(F32) + swap(grads[3], 1).astype(F32)).astype(BF16)
        sums.append(swap(two, 2))
        whole = grads[0].shape[0]
        thin = not all(rows % 16 == 0 for rows in parts_rows)
        spans, at = [], 0
        for rows in parts_rows:
            spans.append((at, rows))
            at += rows * members
        if not thin:
            pieces = combine(sums, ahead_order, spans, members, keep)
        else:
            total = sum(s.astype(F32) for s in sums).astype(BF16)
            pieces = []
            for k in range(members):
                rows = [
                    lax.dynamic_slice_in_dim(total, first + ahead_order[k] * n, n, 0)
                    for first, n in spans
                ]
                pieces.append(jnp.concatenate(rows + [total[keep:]]))
        total = scatter_pieces(pieces, radices)
        found, at = [], 0
        for rows in parts_rows:
            found.append(total[at : at + rows])
            at += rows
        return found, total[at:]

    (up_g, down_g), bias_rows = reduced(
        ffn_grads, (up_weight.shape[0], down_weight.shape[0]), ffn_grads[0].shape[0] - EXTRA
    )
    bias_g = lax.dynamic_slice_in_dim(bias_rows[0], here * up_bias.shape[0], up_bias.shape[0])
    (out_g,), _ = reduced(out_grads, (out_weight.shape[0],), out_grads[0].shape[0])

    acc = ()
    qkv_grads = [None] * 4
    for r in (3, 2, 1, 0):
        qkv, ot, _, lse = heads[r]
        total, qkv_grads[r] = attend_backward(
            live, xt, w[r], cos, sin, qkv, ot, lse, dots[r], acc, seg_len
        )
        acc = (total,)
    seg_mine, norm_vec = leave(seg, resid, total, vec)
    segments_grad = spread(seg_mine, mine, F32)
    (qkv_g,), _ = reduced(qkv_grads, (qkv_weight.shape[0],), width)

    vecs = jnp.concatenate([norm_vec[0:2], ffn_vec[0:2], jnp.zeros((4, width), F32)])
    vecs = vecs + swap(vecs, 1)
    vecs = vecs + swap(vecs, 2)
    vecs = scatter_pieces([vecs] * members, radices)
    vecs = lax.dynamic_slice_in_dim(vecs, here * norm_gain.shape[0], norm_gain.shape[0], 1)

    return (
        block_out,
        segments_grad,
        vecs[0],
        vecs[1],
        qkv_g.reshape(qkv_weight.shape),
        out_g,
        vecs[2],
        vecs[3],
        up_g,
        bias_g,
        down_g,
    )


def solution(mesh):
    placed = (
        P("dp", None, None),
        P("dp", None),
        P("dp"),
        P("dp"),
        P("dp"),
        P("dp", None, "tensor"),
        P(("tensor", "dp"), None),
        P("dp"),
        P("dp"),
        P("dp", "tensor"),
        P(("tensor", "dp")),
        P(("tensor", "dp"), None),
        P("dp", None, None),
    )
    return jax.shard_map(
        local,
        mesh=mesh,
        in_specs=placed,
        out_specs=(
            P("dp", None, None),
            P("dp", None, None),
            P("dp"),
            P("dp"),
            P("dp", None, "tensor"),
            P(("tensor", "dp"), None),
            P("dp"),
            P("dp"),
            P("dp", "tensor"),
            P(("tensor", "dp")),
            P(("tensor", "dp"), None),
        ),
        check_vma=False,
    )
```

```python
import math

import jax
import jax.numpy as jnp
from jax import lax
from jax.experimental import pallas as pl
from jax.experimental.pallas import tpu as pltpu
from jax.sharding import PartitionSpec as P

HEAD = 64
PAIR = 2 * HEAD
BLOCK = 256
EPSILON = 1e-05
MASKED = -1e30
BF16 = jnp.bfloat16
F32 = jnp.float32
EXTRA = 16


def nn(a, b):
    return lax.dot_general(a, b, (((1,), (0,)), ((), ())), preferred_element_type=F32)


def nt(a, b):
    return lax.dot_general(a, b, (((1,), (1,)), ((), ())), preferred_element_type=F32)


def call(kernel, operands, outs, scratch=(), scalars=0, name=None, us=1.0, specs=None):
    inner = [pl.BlockSpec(memory_space=pltpu.SMEM) for _ in range(scalars)]
    inner += [pl.BlockSpec(memory_space=pltpu.VMEM) for _ in operands[scalars:]]
    for at, spec in (specs or {}).items():
        inner[at] = spec
    moved = sum(math.prod(s) * jnp.dtype(d).itemsize for s, d in outs)
    return pl.pallas_call(
        kernel,
        grid=(1,),
        in_specs=inner,
        out_specs=[pl.BlockSpec(memory_space=pltpu.VMEM) for _ in outs],
        out_shape=[jax.ShapeDtypeStruct(s, d) for s, d in outs],
        scratch_shapes=list(scratch),
        compiler_params=pltpu.CompilerParams(vmem_limit_bytes=20 * 1024 * 1024),
        cost_estimate=pl.CostEstimate(
            flops=int(us * 1.1e9), bytes_accessed=int(min(2 * moved, us * 3e6)), transcendentals=0
        ),
        name=name,
    )(*operands)


def bits_of(size):
    assert size & (size - 1) == 0
    return [size >> (k + 1) for k in range(size.bit_length() - 1)]


def across(value, bit):
    return lax.ppermute(value, "dp", [(i, i ^ bit) for i in range(lax.axis_size("dp"))])


def joined(arrays):
    return arrays[0] if len(arrays) == 1 else jnp.concatenate(arrays)


def widened(arrays, order, bit, step=across):
    whole = joined(arrays)
    return [whole, step(whole, bit)], order + [o ^ bit for o in order]


def halving_order(bits):
    order = [0]
    for bit in reversed(bits):
        order = order + [o ^ bit for o in order]
    return order


def swap(value, bit):
    return lax.ppermute(value, "tensor", [(t, t ^ bit) for t in range(lax.axis_size("tensor"))])


def gate(value, *earlier):
    return lax.optimization_barrier((value, *earlier))


class Held:
    def __init__(self, kept):
        self.kept = kept


class Halving(Held):
    def __init__(self, halves, steps):
        self.kept, self.sent = halves
        self.steps = list(steps)

    def step(self, *earlier):
        (move, bit), *self.steps = self.steps
        got, *kept = gate(move(self.sent, bit), *(e.kept for e in earlier))
        for e, k in zip(earlier, kept):
            e.kept = k
        if self.steps:
            half = self.kept.shape[0] // 2
            parts = [slice(None, half), slice(half, None)]
            self.kept, self.sent = (
                (self.kept[p].astype(F32) + got[p].astype(F32)).astype(BF16) for p in parts
            )
        else:
            self.kept, self.sent = self.kept[0].astype(F32) + got[0].astype(F32), None
        return self


def in_place(arrays, order, parts):
    if all(rows % 16 == 0 for rows in parts):
        return arrays, order, parts
    count = order.shape[0]
    stacked = joined(arrays)
    where = jnp.zeros((count,), jnp.int32).at[order].set(jnp.arange(count, dtype=jnp.int32))
    stacked = stacked[where]
    laid, at = [], 0
    for rows in parts:
        laid.append(stacked[:, at : at + rows].reshape(count * rows, -1))
        at += rows
    if at < stacked.shape[1]:
        laid.append(stacked[:, at:].astype(F32).sum(axis=0).astype(stacked.dtype))
    whole = jnp.concatenate(laid)[None]
    return [whole], jnp.zeros((1,), jnp.int32), [count * r for r in parts]


def norm_parts(rows):
    centred = rows - jnp.mean(rows, axis=-1, keepdims=True)
    rstd = lax.rsqrt(jnp.mean(centred * centred, axis=-1, keepdims=True) + EPSILON)
    return centred * rstd, rstd


def norm_pull(grad, gain, xhat, rstd):
    scaled = grad * gain
    level = jnp.mean(scaled, axis=-1, keepdims=True)
    along = jnp.mean(scaled * xhat, axis=-1, keepdims=True)
    return rstd * (scaled - level - xhat * along)


def colsum(rows):
    return jnp.sum(rows, axis=0, keepdims=True)


def each_piece(refs):
    k = 0
    for ref in refs:
        for j in range(ref.shape[0]):
            yield k, ref, j
            k += 1


def enter(seg, arrays, order, rows, seg_len, padded, width, cols):
    count = len(arrays)

    def kernel(order_ref, seg_ref, *refs):
        parts = refs[:count]
        w_out, xt_out, vec_out, x_scr = refs[count:]
        vec = 0.0
        for k, ref, j in each_piece(parts):
            start = pl.multiple_of(order_ref[k] * rows, 16)
            w_out[pl.ds(start, rows), :] = ref[j, 0:rows, :]
            vec = vec + ref[j, rows:, :].astype(F32)
        w_out[width:, :] = vec.astype(BF16)
        vec_out[...] = jnp.zeros(vec_out.shape, F32)
        for v in range(4):
            vec_out[v : v + 1, 0:cols] = vec[2 * v : 2 * v + 1, :]
            vec_out[v : v + 1, cols:width] = vec[2 * v + 1 : 2 * v + 2, 0 : width - cols]
        gain = vec_out[0:1, :]
        shift = vec_out[1:2, :]
        step = seg_len // 4

        def body(c, carry):
            at = pl.multiple_of(c * step, 16)
            xhat, _ = norm_parts(seg_ref[pl.ds(at, step), :].astype(F32))
            x_scr[pl.ds(at, step), :] = (xhat * gain + shift).astype(BF16)
            return carry

        lax.fori_loop(0, 4, body, 0)
        x_scr[seg_len:padded, :] = jnp.zeros((padded - seg_len, width), BF16)
        xt_out[...] = x_scr[...].T

    return call(
        kernel,
        (order, seg, *arrays),
        [((width + EXTRA, cols), BF16), ((width, padded), BF16), ((8, width), F32)],
        [pltpu.VMEM((padded, width), BF16)],
        scalars=1,
        name="enter",
        us=2.0,
    )


def lay_out(first, second, orders, parts, w, width):
    n_first, n_second = len(first), len(second)
    (out_rows, up_rows), (down_rows,) = parts
    cols = w.shape[1]
    counts = [sum(a.shape[0] for a in first), sum(a.shape[0] for a in second)]
    up_at = counts[0] * out_rows
    down_at = up_at + counts[0] * up_rows
    bias_at = down_at + counts[1] * down_rows

    def kernel(first_order, second_order, w_ref, *refs):
        wide = refs[-1]
        for k, ref, j in each_piece(refs[:n_first]):
            o = first_order[k]
            wide[pl.ds(pl.multiple_of(o * out_rows, 16), out_rows), :] = ref[j, 0:out_rows, :]
            start = pl.multiple_of(up_at + o * up_rows, 16)
            wide[pl.ds(start, up_rows), :] = ref[j, out_rows:, :]
        for k, ref, j in each_piece(refs[n_first : n_first + n_second]):
            start = pl.multiple_of(down_at + second_order[k] * down_rows, 16)
            wide[pl.ds(start, down_rows), :] = ref[j]
        bias = jnp.concatenate([w_ref[8:9, :], w_ref[9:10, 0 : width - cols]], axis=1)
        wide[bias_at:, :] = jnp.broadcast_to(bias, (EXTRA, width))

    return call(
        kernel,
        (*orders, w, *first, *second),
        [((bias_at + EXTRA, width), BF16)],
        scalars=2,
        name="lay_out",
        us=1.0,
        specs={2: pl.BlockSpec((EXTRA, cols), lambda i: (width // EXTRA, 0))},
    )[0]


def blocks_of(seg_len):
    return [(s, min(s + BLOCK, seg_len)) for s in range(0, seg_len, BLOCK)]


def one_head(block, h):
    row = lax.broadcasted_iota(jnp.int32, block.shape, 0)
    return jnp.where(row // HEAD == h, block, jnp.zeros_like(block))


def allowed_slots(live, start, stop):
    place = lax.broadcasted_iota(jnp.int32, (1, BLOCK), 1) + start
    bound = jnp.minimum(place, live - 1)
    return lax.broadcasted_iota(jnp.int32, (stop, BLOCK), 0) <= bound


def attend_forward(live, xt, w, cos, sin, seg_len):
    width, padded = xt.shape
    half = HEAD // 2

    def kernel(live_ref, xt_ref, w_ref, cos_ref, sin_ref, qkv_out, ot_out, mixed_out, lse_out):
        proj = nn(w_ref[0:width, :].T, xt_ref[...])
        cosine = cos_ref[...]
        sine = sin_ref[...]

        def rot(z):
            a, b = z[0:half], z[half:]
            return jnp.concatenate([a * cosine - b * sine, b * cosine + a * sine], axis=0)

        for h in range(2):
            r = h * HEAD
            qkv_out[r : r + HEAD, :] = (rot(proj[r : r + HEAD]) * HEAD ** (-0.5)).astype(BF16)
            r = r + PAIR
            qkv_out[r : r + HEAD, :] = rot(proj[r : r + HEAD]).astype(BF16)
        qkv_out[2 * PAIR :, :] = proj[2 * PAIR :].astype(BF16)
        keys = qkv_out[PAIR : 2 * PAIR, :].T
        lse_out[...] = jnp.zeros(lse_out.shape, F32)
        def head(h, carry):
            r = pl.multiple_of(h * HEAD, HEAD)
            for start, stop in blocks_of(seg_len):
                cols = slice(start, start + BLOCK)
                allowed = allowed_slots(live_ref[0], start, stop)
                query = one_head(qkv_out[0:PAIR, cols], h)
                scores = jnp.where(allowed, nn(keys[0:stop], query), MASKED)
                top = jnp.max(scores, axis=0, keepdims=True)
                weights = jnp.exp(scores - top)
                total = colsum(weights)
                probs = (weights * (1.0 / total)).astype(BF16)
                value = qkv_out[pl.ds(2 * PAIR + r, HEAD), 0:stop]
                ot_out[pl.ds(r, HEAD), cols] = nn(value, probs).astype(BF16)
                lse_out[pl.ds(h, 1), cols] = top + jnp.log(total)
            return carry

        lax.fori_loop(0, 2, head, 0)
        mixed_out[...] = ot_out[...].T[0:seg_len]

    return call(
        kernel,
        (live, xt, w, cos, sin),
        [
            ((3 * PAIR, padded), BF16),
            ((PAIR, padded), BF16),
            ((seg_len, PAIR), BF16),
            ((8, padded), F32),
        ],
        scalars=1,
        name="attend_forward",
        us=4.0,
    )


def emit(cut, order_ref, kept, sent):
    half = kept.shape[0]
    for k in range(2 * half):
        target, j = (kept, k) if k < half else (sent, k - half)
        cut(order_ref[k], target.at[j])


def attend_backward(live, xt, w, cos, sin, qkv, ot, lse, dot, acc, seg_len):
    width, padded = xt.shape
    half = HEAD // 2
    n_acc = len(acc)

    def kernel(live_ref, xt_ref, w_ref, cos_ref, sin_ref, qkv_ref, ot_ref, lse_ref, dot_ref, *refs):
        acc_refs = refs[:n_acc]
        acc_out, grad_out, d_scr, pg_scr, inner_scr = refs[n_acc:]
        cosine = cos_ref[...]
        sine = sin_ref[...]
        keys = qkv_ref[PAIR : 2 * PAIR, :].T
        values = qkv_ref[2 * PAIR :, :].T
        prod = dot_ref[...].astype(F32) * ot_ref[...].astype(F32)
        d_scr[...] = jnp.zeros(d_scr.shape, F32)
        for h in range(2):
            inner_scr[h : h + 1, :] = colsum(prod[h * HEAD : h * HEAD + HEAD])

        def head(h, carry):
            r = pl.multiple_of(h * HEAD, HEAD)
            q_at, k_at, v_at = (pl.ds(part * PAIR + r, HEAD) for part in range(3))
            for start, stop in blocks_of(seg_len):
                cols = slice(start, start + BLOCK)
                allowed = allowed_slots(live_ref[0], start, stop)
                query = one_head(qkv_ref[0:PAIR, cols], h)
                scores = jnp.where(allowed, nn(keys[0:stop], query), MASKED)
                probs = jnp.exp(scores - lse_ref[pl.ds(h, 1), cols])
                prob_grad = nn(values[0:stop], one_head(dot_ref[:, cols], h))
                score_grad = (probs * (prob_grad - inner_scr[pl.ds(h, 1), cols])).astype(BF16)
                d_scr[q_at, cols] = nn(qkv_ref[k_at, 0:stop], score_grad)
                d_scr[k_at, 0:stop] += nt(qkv_ref[q_at, cols], score_grad)
                d_scr[v_at, 0:stop] += nt(dot_ref[pl.ds(r, HEAD), cols], probs.astype(BF16))
            return carry

        lax.fori_loop(0, 2, head, 0)

        def unrot(z):
            a, b = z[0:half], z[half:]
            return jnp.concatenate([a * cosine + b * sine, b * cosine - a * sine], axis=0)

        for h in range(2):
            r = h * HEAD
            pg_scr[r : r + HEAD, :] = (unrot(d_scr[r : r + HEAD, :]) * HEAD ** (-0.5)).astype(BF16)
            r = r + PAIR
            pg_scr[r : r + HEAD, :] = unrot(d_scr[r : r + HEAD, :]).astype(BF16)
        pg_scr[2 * PAIR :, :] = d_scr[2 * PAIR :, :].astype(BF16)
        part = nn(w_ref[0:width, :], pg_scr[...])
        acc_out[...] = acc_refs[0][...] + part if n_acc else part
        grad_out[...] = nt(xt_ref[...], pg_scr[...]).astype(BF16)

    return call(
        kernel,
        (live, xt, w, cos, sin, qkv, ot, lse, dot, *acc),
        [((width, padded), F32), ((width, 3 * PAIR), BF16)],
        [
            pltpu.VMEM((3 * PAIR, padded), F32),
            pltpu.VMEM((3 * PAIR, padded), BF16),
            pltpu.VMEM((8, padded), F32),
        ],
        scalars=1,
        name="attend_backward",
        us=1.0,
    )


def rows_of(whole, first, index, rows):
    return whole[pl.ds(pl.multiple_of(first + index * rows, 16), rows), :]


def halves_call(kernel, operands, count, rows, cols, scratch, name):
    return call(
        kernel,
        operands,
        [((count // 2, rows, cols), BF16)] * 2,
        scratch,
        scalars=1,
        name=name,
        us=1.5,
    )


def cut_heads(grads, vec, order, rows):
    whole_rows, cols = grads[0].shape
    width = vec.shape[1]
    count = order.shape[0]

    def kernel(order_ref, a_ref, b_ref, c_ref, vec_ref, kept, sent, whole):
        whole[...] = (a_ref[...].astype(F32) + b_ref[...].astype(F32) + c_ref[...].astype(F32)).astype(BF16)
        tail = jnp.zeros((EXTRA - 4, cols), F32)
        blank = jnp.zeros((1, 2 * cols - width), F32)
        v0, v1 = vec_ref[0:1, :], vec_ref[1:2, :]
        parts = []
        for v in (v0, v1):
            parts.append(v[:, 0:cols])
            parts.append(jnp.concatenate([v[:, cols:width], blank], axis=1))
        last = jnp.concatenate(parts + [tail], axis=0).astype(BF16)

        def cut(index, piece):
            piece[0:rows, :] = rows_of(whole, 0, index, rows)
            piece[rows:, :] = last

        emit(cut, order_ref, kept, sent)

    return halves_call(
        kernel,
        (order, *grads, vec),
        count,
        rows + EXTRA,
        cols,
        [pltpu.VMEM((whole_rows, cols), BF16)],
        "cut_heads",
    )


def cut_down(downs, outs, out_near, order, down_rows, out_rows):
    width = downs[0].shape[1]
    count = order.shape[0]
    down = down_rows * count
    tall = out_rows * count + EXTRA
    end = down + tall - EXTRA

    def kernel(order_ref, *refs):
        down_refs, out_refs = refs[0:2], refs[2:4]
        near_ref, kept, sent = refs[4:7]
        wholes = refs[7:9]
        for side, whole in enumerate(wholes):
            near = near_ref[side * tall : (side + 1) * tall, :].astype(F32)
            outs_sum = out_refs[side][...].astype(F32) + near
            whole[0 : tall - EXTRA, :] = outs_sum[0 : tall - EXTRA].astype(BF16)
            bias = down_refs[side][down:, :].astype(F32)
            whole[tall - EXTRA :, :] = (outs_sum[tall - EXTRA :] + bias).astype(BF16)
        half = kept.shape[0]
        for k in range(count):
            for side, whole in enumerate(wholes):
                j = 2 * k + side
                target, j = (kept, j) if j < half else (sent, j - half)
                index = order_ref[k]
                target[j, 0:down_rows, :] = rows_of(down_refs[side], 0, index, down_rows)
                target[j, down_rows : down_rows + out_rows, :] = rows_of(whole, 0, index, out_rows)
                target[j, down_rows + out_rows :, :] = whole[tall - EXTRA :, :]

    return halves_call(
        kernel,
        (order, *downs, *outs, out_near),
        2 * count,
        down_rows + out_rows + EXTRA,
        width,
        [pltpu.VMEM((tall, width), BF16)] * 2,
        "cut_down",
    )


def cut_up(grads, order, rows):
    height, width = grads[0].shape
    count = order.shape[0]
    whole_rows = rows * count

    def kernel(order_ref, a_ref, b_ref, c_ref, d_ref, kept, sent, rest_near, rest_far, near, far):
        here = slice(0, whole_rows)
        rest = slice(whole_rows, height)
        for x_ref, y_ref, up, other in ((a_ref, b_ref, near, rest_near), (c_ref, d_ref, far, rest_far)):
            up[...] = (x_ref[here, :].astype(F32) + y_ref[here, :].astype(F32)).astype(BF16)
            other[...] = (x_ref[rest, :].astype(F32) + y_ref[rest, :].astype(F32)).astype(BF16)
        half = kept.shape[0]
        for k in range(count):
            for side, whole in enumerate((near, far)):
                j = 2 * k + side
                target, j = (kept, j) if j < half else (sent, j - half)
                target[j] = rows_of(whole, 0, order_ref[k], rows)

    kept, sent, *rest = call(
        kernel,
        (order, *grads),
        [((count, rows, width), BF16)] * 2 + [((height - whole_rows, width), BF16)] * 2,
        [pltpu.VMEM((whole_rows, width), BF16)] * 2,
        scalars=1,
        name="cut_up",
        us=1.5,
    )
    return (kept, sent), rest


def cut_thin(totals, order, spans, last):
    pieces = []
    for k in range(order.shape[0]):
        for total in totals:
            piece = [
                lax.dynamic_slice_in_dim(total, first + order[k] * rows, rows, 0)
                for first, rows in spans
            ]
            pieces.append(jnp.concatenate(piece + ([total[-EXTRA:]] if last is None else last)))
    pieces = jnp.stack(pieces)
    half = pieces.shape[0] // 2
    return pieces[:half], pieces[half:]


def added(arrays):
    return sum(a.astype(F32) for a in arrays).astype(BF16)


def merge_attention(seg, mixed, outs, vec):
    rows, width = seg.shape
    n = len(mixed)

    def kernel(seg_ref, vec_ref, *refs):
        mixed_refs, out_refs = refs[:n], refs[n : 2 * n]
        res_out, ffn_out = refs[2 * n :]
        gain = vec_ref[2:3, :]
        shift = vec_ref[3:4, :]
        step = rows // 2

        def body(c, carry):
            at = pl.multiple_of(c * step, 16)
            here = pl.ds(at, step)
            total = nn(mixed_refs[0][here, :], out_refs[0][...])
            for r in range(1, n):
                total = total + nn(mixed_refs[r][here, :], out_refs[r][...])
            total = total + seg_ref[here, :].astype(F32)
            res_out[here, :] = total
            xhat, _ = norm_parts(total)
            ffn_out[here, :] = (xhat * gain + shift).astype(BF16)
            return carry

        lax.fori_loop(0, 2, body, 0)

    return call(
        kernel,
        (seg, vec, *mixed, *outs),
        [((rows, width), F32), ((rows, width), BF16)],
        name="merge_attention",
        us=2.0,
        specs={2 + n + r: pl.BlockSpec((PAIR, width), lambda i: (0, 0)) for r in range(n)},
    )


def feed_forward(ffn_in, cot, wide, acc):
    rows, width = ffn_in.shape
    units = (wide.shape[0] - EXTRA - PAIR) // 2
    up_at, down_at, bias_at = PAIR, PAIR + units, PAIR + 2 * units
    n_acc = len(acc)

    def kernel(x_ref, cot_ref, ud_ref, *refs):
        acc_refs = refs[:n_acc]
        out_acc, back_acc, grad_out, act_scr, pg_scr = refs[n_acc:]
        step = rows // 2
        bias = ud_ref[bias_at : bias_at + 1, :].astype(F32)

        def body(c, total):
            at = pl.multiple_of(c * step, 16)
            here = pl.ds(at, step)
            up = ud_ref[up_at:down_at, :]
            down = ud_ref[down_at:bias_at, :]
            pre = nn(x_ref[here, :], up) + bias
            below = 0.5 + 0.5 * lax.erf(pre * 0.5**0.5)
            act = (pre * below).astype(BF16)
            slope = below + pre * (jnp.exp(-0.5 * (pre * pre)) * (1.0 / math.sqrt(2.0 * math.pi)))
            pre_grad = (nt(cot_ref[here, :], down) * slope).astype(BF16)
            act_scr[here, :] = act
            pg_scr[here, :] = pre_grad
            fwd = nn(act, down)
            back = nt(pre_grad, up)
            if n_acc:
                fwd = fwd + acc_refs[0][here, :]
                back = back + acc_refs[1][here, :]
            out_acc[here, :] = fwd
            back_acc[here, :] = back
            return total + colsum(pre_grad.astype(F32))

        total = lax.fori_loop(0, 2, body, jnp.zeros((1, units), F32))
        grad_out[0:units, :] = nn(x_ref[...].T, pg_scr[...]).astype(BF16)
        grad_out[units : 2 * units, :] = nn(act_scr[...].T, cot_ref[...]).astype(BF16)
        last = jnp.concatenate([total, jnp.zeros((EXTRA - 1, units), F32)], axis=0)
        grad_out[2 * units :, :] = last.astype(BF16)

    return call(
        kernel,
        (ffn_in, cot, wide, *acc),
        [((rows, width), F32), ((rows, width), F32), ((2 * units + EXTRA, width), BF16)],
        [pltpu.VMEM((rows, units), BF16), pltpu.VMEM((rows, units), BF16)],
        name="feed_forward",
        us=3.0,
    )


def turn_back(res, forward, backward, cot, vec, mixed_t, wides, padded):
    rows, width = res.shape
    n = len(wides)
    out_rows = PAIR + EXTRA

    def kernel(res_ref, fwd_ref, back_ref, cot_ref, vec_ref, *refs):
        mixed_refs, out_refs = refs[:n], refs[n : 2 * n]
        block_out, resid_out, own_out, other_out, near_out = refs[2 * n : 2 * n + 5]
        dot_outs = refs[2 * n + 5 : 3 * n + 5]
        low_scr = refs[-1]
        gain = vec_ref[2:3, :]
        step = rows // 4

        def body(c, sums):
            here = pl.ds(pl.multiple_of(c * step, 16), step)
            res_rows = res_ref[here, :]
            back = back_ref[here, :]
            block_out[here, :] = (res_rows + fwd_ref[here, :]).astype(BF16)
            xhat, rstd = norm_parts(res_rows)
            resid = cot_ref[here, :].astype(F32) + norm_pull(back, gain, xhat, rstd)
            resid_out[here, :] = resid
            low_scr[here, :] = resid.astype(BF16)
            return sums[0] + colsum(back * xhat), sums[1] + colsum(back)

        zero = jnp.zeros((1, width), F32)
        gain_grad, shift_grad = lax.fori_loop(0, 4, body, (zero, zero))
        last = [zero, gain_grad, shift_grad, jnp.zeros((EXTRA - 3, width), F32)]
        last = jnp.concatenate(last, axis=0).astype(BF16)
        low_scr[rows:, :] = jnp.zeros((padded - rows, width), BF16)
        places = [(own_out, 0), (near_out, 0), (other_out, 0), (near_out, out_rows)]
        for r, (target, at) in enumerate(places):
            dot_outs[r][...] = nt(out_refs[r][...], low_scr[...]).astype(BF16)
            grad = nn(mixed_refs[r][...], low_scr[...]).astype(BF16)
            target[at : at + PAIR, :] = grad
            target[at + PAIR : at + out_rows, :] = last

    return call(
        kernel,
        (res, forward, backward, cot, vec, *mixed_t, *wides),
        [((rows, width), BF16), ((rows, width), F32)]
        + [((out_rows, width), BF16)] * 2
        + [((2 * out_rows, width), BF16)]
        + [((PAIR, padded), BF16)] * n,
        [pltpu.VMEM((padded, width), BF16)],
        name="turn_back",
        us=0.5,
        specs={5 + n + r: pl.BlockSpec((PAIR, width), lambda i: (0, 0)) for r in range(n)},
    )


def leave(seg, resid, acc, vec):
    rows, width = seg.shape
    padded = acc.shape[1]

    def kernel(seg_ref, resid_ref, acc_ref, vec_ref, seg_out, vec_out, acc_scr):
        gain = vec_ref[0:1, :]
        step = rows // 4
        acc_scr[...] = acc_ref[...].T

        def body(c, sums):
            here = pl.ds(pl.multiple_of(c * step, 16), step)
            grad = acc_scr[here, :]
            xhat, rstd = norm_parts(seg_ref[here, :].astype(F32))
            seg_out[here, :] = (resid_ref[here, :] + norm_pull(grad, gain, xhat, rstd)).astype(BF16)
            return sums[0] + colsum(grad * xhat), sums[1] + colsum(grad)

        zero = jnp.zeros((1, width), F32)
        gain_grad, shift_grad = lax.fori_loop(0, 4, body, (zero, zero))
        vec_out[...] = jnp.zeros(vec_out.shape, F32)
        vec_out[0:1, :] = gain_grad
        vec_out[1:2, :] = shift_grad

    return call(
        kernel,
        (seg, resid, acc, vec),
        [((rows, width), BF16), ((8, width), F32)],
        [pltpu.VMEM((padded, width), F32)],
        name="leave",
        us=0.5,
    )


def spread(mine, other, tensor_index, dtype):
    rows, width = mine.shape
    parts = [mine, swap(mine, 1), other, swap(other, 1)]

    def kernel(index_ref, *refs):
        out = refs[-1]
        for r, ref in enumerate(refs[:-1]):
            @pl.when(pl.program_id(0) == r)
            def _():
                out[0] = ref[...].astype(dtype)

    return pl.pallas_call(
        kernel,
        grid_spec=pltpu.PrefetchScalarGridSpec(
            num_scalar_prefetch=1,
            grid=(len(parts),),
            in_specs=[pl.BlockSpec((rows, width), lambda i, t: (0, 0)) for _ in parts],
            out_specs=pl.BlockSpec((1, rows, width), lambda i, t: (t[0] ^ i, 0, 0)),
        ),
        out_shape=jax.ShapeDtypeStruct((len(parts), rows, width), dtype),
        compiler_params=pltpu.CompilerParams(vmem_limit_bytes=24 * 1024 * 1024),
        name="spread",
    )(jnp.reshape(tensor_index, (1,)).astype(jnp.int32), *parts)


def own_shares(norm_vecs, ffn_vecs, place, share):
    width = ffn_vecs.shape[1]
    cols = norm_vecs.shape[1]

    def kernel(place_ref, norm_ref, ffn_ref, *outs):
        whole = jnp.concatenate([norm_ref[0:2, 0:width], ffn_ref[0:8, :]], axis=0)
        total = jnp.zeros((whole.shape[0], share), F32)
        for k in range(width // share):
            part = whole[:, k * share : (k + 1) * share]
            total = total + jnp.where(place_ref[0] == k, part, jnp.zeros_like(part))
        for v, out in enumerate(outs):
            out[...] = total[v : v + 1]

    outs = call(
        kernel,
        (jnp.reshape(place, (1,)).astype(jnp.int32), norm_vecs, ffn_vecs),
        [((1, share), F32)] * 5,
        scalars=1,
        name="own_shares",
    )
    return [o.reshape(share) for o in outs]


def rotary_tables(starts, padded):
    half = HEAD // 2
    inverse = jnp.exp(jnp.arange(half).astype(F32) * (-math.log(10000.0) / half))
    angles = inverse[:, None] * starts.astype(F32)[None, :]
    angles = jnp.pad(angles, ((0, 0), (0, padded - starts.shape[0])))
    return jnp.cos(angles), jnp.sin(angles)


def vector_rows(vectors, here, width, cols):
    own = vectors[0].shape[0]
    tiled = jnp.concatenate([jnp.tile(v, 2 * cols // own).reshape(2, cols) for v in vectors])
    tiled = jnp.pad(tiled, ((0, EXTRA - tiled.shape[0]), (0, 0)))
    row = lax.broadcasted_iota(jnp.int32, tiled.shape, 0)
    place = lax.broadcasted_iota(jnp.int32, tiled.shape, 1) + row % 2 * cols
    return jnp.where(place // own == here, tiled, jnp.zeros_like(tiled))


def local(
    segments,
    seg_start,
    seg_count,
    norm_gain,
    norm_shift,
    qkv_weight,
    out_weight,
    ffn_gain,
    ffn_shift,
    up_weight,
    up_bias,
    down_weight,
    cotangent,
):
    seq_local, seg_len, width = segments.shape
    tensor = lax.axis_size("tensor")
    members = lax.axis_size("dp")
    assert seq_local == tensor == 4
    padded = -(-seg_len // BLOCK) * BLOCK
    bits = bits_of(members)
    here = lax.axis_index("dp")
    mine = lax.axis_index("tensor")
    cols = 3 * qkv_weight.shape[2]
    assert cols == 3 * PAIR and width * 2 > cols
    groups = range(tensor)
    thin = any(
        a.shape[0] % 16 for a in (qkv_weight, out_weight, up_weight, down_weight)
    )

    seg = lax.dynamic_index_in_dim(segments, mine, 0, keepdims=False)
    cot = lax.dynamic_index_in_dim(cotangent, mine, 0, keepdims=False)
    starts = lax.dynamic_index_in_dim(seg_start, mine, 0, keepdims=False)
    live = lax.dynamic_slice_in_dim(seg_count, mine, 1)
    cos, sin = rotary_tables(starts, padded)

    def indices(distances):
        return here ^ jnp.asarray(distances, jnp.int32)

    qkv_rows, out_rows = qkv_weight.shape[0], out_weight.shape[0]
    up_rows, down_rows = up_weight.shape[0], down_weight.shape[0]
    vectors = (norm_gain, norm_shift, ffn_gain, ffn_shift, up_bias)
    first = jnp.concatenate(
        [qkv_weight.reshape(-1, cols), vector_rows(vectors, here, width, cols)]
    )
    arrays, order = [first[None]], [0]
    side, side_order = [jnp.concatenate([out_weight, up_weight])[None]], [0]
    down, down_order = [down_weight[None]], [0]
    for bit in bits[:-1]:
        arrays, order = widened(arrays, order, bit)
        side, side_order = widened(side, side_order, bit)
        down, down_order = widened(down, down_order, bit)
    arrays, order = widened(arrays, order, bits[-1])
    side, side_order = widened(side, side_order, bits[-1])
    down = joined(down)
    down = [down, swap(down, 2)]
    down_far = [across(d, bits[-1]) for d in down]
    down_order = down_order + [o ^ bits[-1] for o in down_order]

    pieces, places, parts = in_place(arrays, indices(order), (qkv_rows,))
    w0, xt, vec = enter(seg, pieces, places, parts[0], seg_len, padded, width, cols)
    w = [w0, swap(w0, 1), swap(w0, 2), None]
    w[3] = swap(w[2], 1)
    wides = []
    sides = [side, [swap(s, 2) for s in side]]
    for r in range(2):
        s, s_places, s_parts = in_place(sides[r], indices(side_order), (out_rows, up_rows))
        d, d_places, d_parts = in_place([down[r], down_far[r]], indices(down_order), (down_rows,))
        wide = lay_out(s, d, (s_places, d_places), (s_parts, d_parts), w[2 * r], width)
        wides += [wide, swap(wide, 1)]

    heads = [attend_forward(live, xt, w[r], cos, sin, seg_len) for r in groups]
    res, ffn_in = merge_attention(seg, [h[2] for h in heads], wides, vec)
    back_bits = bits[::-1]
    dp_steps = [(across, b) for b in back_bits]
    ahead = indices(halving_order(back_bits))
    acc = ()
    ffn_grads = [None] * 4
    for r in (3, 2, 1, 0):
        out_acc, back_acc, ffn_grads[r] = feed_forward(ffn_in, cot, wides[r], acc)
        acc = (out_acc, back_acc)
    ups = (ffn_grads[0], swap(ffn_grads[1], 1), ffn_grads[2], swap(ffn_grads[3], 1))
    units = (ffn_grads[0].shape[0] - EXTRA) // 2
    if thin:
        up_halves = cut_thin(
            [added([ups[0], ups[1]])[:width], added([ups[2], ups[3]])[:width]],
            ahead, [(0, up_rows)], [],
        )
    else:
        up_halves, downs = cut_up(ups, ahead, up_rows)
    res, up_halves = lax.optimization_barrier((res, up_halves))
    turned = turn_back(res, *acc, cot, vec, [h[1] for h in heads], wides, padded)
    block_mine, resid, out_own, out_other, out_near = turned[0:5]
    dots = list(turned[5:9])
    block_out = spread(block_mine, swap(block_mine, 2), mine, BF16)
    out_near = swap(out_near, 1)
    if thin:
        down_totals = []
        for side, own_out in enumerate((out_own, out_other)):
            tall = own_out.shape[0]
            out_sum = own_out.astype(F32) + out_near[side * tall : (side + 1) * tall].astype(F32)
            ffn_sum = added([ups[2 * side][units:], ups[2 * side + 1][units:]])
            last = out_sum[-EXTRA:] + ffn_sum[-EXTRA:].astype(F32)
            down_totals.append(
                jnp.concatenate([ffn_sum[:-EXTRA], out_sum[:-EXTRA].astype(BF16), last.astype(BF16)])
            )
        down_halves = cut_thin(
            down_totals, ahead, [(0, down_rows), (units, out_rows)], None
        )
    else:
        down_halves = cut_down(downs, (out_own, out_other), out_near, ahead, down_rows, out_rows)
    up = Halving(up_halves, dp_steps + [(swap, 2)])
    down = Halving(down_halves, dp_steps + [(swap, 2)])

    acc = ()
    qkv_grads = [None] * 4
    for r in (3, 2, 1, 0):
        if r == 2:
            up.step()
            dots[r], up.kept, up.sent, down.kept, down.sent = gate(
                dots[r], up.kept, up.sent, down.kept, down.sent
            )
        if r == 1:
            up.step()
            dots[r], up.kept, up.sent, other = gate(dots[r], up.kept, up.sent, other)
        qkv, ot, _, lse = heads[r]
        total, qkv_grads[r] = attend_backward(
            live, xt, w[r], cos, sin, qkv, ot, lse, dots[r], acc, seg_len
        )
        acc = (total,)
        if r == 2:
            other = added([qkv_grads[2], swap(qkv_grads[3], 1)])
    seg_mine, norm_vec = leave(seg, resid, total, vec)
    seg_mine = Held(seg_mine)
    down.step(seg_mine)
    up.step(down)
    other = swap(other, 2)
    other, up.kept = gate(other, up.kept)
    parts = (qkv_grads[0], swap(qkv_grads[1], 1), other)
    if thin:
        last = jnp.pad(norm_vec[0:2], ((0, 0), (0, 2 * cols - width))).reshape(4, cols)
        last = jnp.pad(last, ((0, EXTRA - 4), (0, 0))).astype(BF16)
        qkv_halves = cut_thin([added(parts)], ahead, [(0, qkv_rows)], [last])
    else:
        qkv_halves = cut_heads(parts, norm_vec, ahead, qkv_rows)
    heads_sum = Halving(qkv_halves, dp_steps)
    previous, seg_other = heads_sum, Held(swap(seg_mine.kept, 2))
    sums = (down, up, heads_sum)
    turns = 0
    while any(part.steps for part in sums):
        for part in sums:
            if part.steps:
                part.step(previous)
                previous = part
        turns += 1
        if turns == 2:
            seg_other.kept, previous.kept = gate(seg_other.kept, previous.kept)
            segments_grad = spread(seg_mine.kept, seg_other.kept, mine, F32)
    up_g, total_down, total = up.kept, down.kept, heads_sum.kept
    down_g = total_down[0:down_rows]
    out_g = total_down[down_rows : down_rows + out_rows]
    ffn_vecs = total_down[down_rows + out_rows :]
    qkv_g = total[0:qkv_rows]
    norm_vecs = total[qkv_rows : qkv_rows + 4].reshape(2, 2 * cols)
    norm_vecs = norm_vecs + swap(norm_vecs, 1)
    norm_vecs = norm_vecs + swap(norm_vecs, 2)

    share = norm_gain.shape[0]
    assert up_bias.shape[0] == share
    norm_gain_g, norm_shift_g, bias_g, ffn_gain_g, ffn_shift_g = own_shares(
        norm_vecs, ffn_vecs, here, share
    )
    return (
        block_out,
        segments_grad,
        norm_gain_g,
        norm_shift_g,
        qkv_g.reshape(qkv_weight.shape),
        out_g,
        ffn_gain_g,
        ffn_shift_g,
        up_g,
        bias_g,
        down_g,
    )


def solution(mesh):
    placed = (
        P("dp", None, None),
        P("dp", None),
        P("dp"),
        P("dp"),
        P("dp"),
        P("dp", None, "tensor"),
        P(("tensor", "dp"), None),
        P("dp"),
        P("dp"),
        P("dp", "tensor"),
        P(("tensor", "dp")),
        P(("tensor", "dp"), None),
        P("dp", None, None),
    )
    return jax.shard_map(
        local,
        mesh=mesh,
        in_specs=placed,
        out_specs=(
            P("dp", None, None),
            P("dp", None, None),
            P("dp"),
            P("dp"),
            P("dp", None, "tensor"),
            P(("tensor", "dp"), None),
            P("dp"),
            P("dp"),
            P("dp", "tensor"),
            P(("tensor", "dp")),
            P(("tensor", "dp"), None),
        ),
        check_vma=False,
    )
```

```python
import math

import jax
import jax.numpy as jnp
from jax import lax
from jax.experimental import pallas as pl
from jax.experimental.pallas import tpu as pltpu
from jax.sharding import PartitionSpec as P

HEAD = 64
PAIR = 2 * HEAD
BLOCK = 256
EPSILON = 1e-05
MASKED = -1e30
BF16 = jnp.bfloat16
F32 = jnp.float32
EXTRA = 16


def nn(a, b):
    return lax.dot_general(a, b, (((1,), (0,)), ((), ())), preferred_element_type=F32)


def nt(a, b):
    return lax.dot_general(a, b, (((1,), (1,)), ((), ())), preferred_element_type=F32)


def call(kernel, operands, outs, scratch=(), scalars=0, name=None, us=1.0, specs=None):
    inner = [pl.BlockSpec(memory_space=pltpu.SMEM) for _ in range(scalars)]
    inner += [pl.BlockSpec(memory_space=pltpu.VMEM) for _ in operands[scalars:]]
    for at, spec in (specs or {}).items():
        inner[at] = spec
    moved = sum(math.prod(s) * jnp.dtype(d).itemsize for s, d in outs)
    return pl.pallas_call(
        kernel,
        grid=(1,),
        in_specs=inner,
        out_specs=[pl.BlockSpec(memory_space=pltpu.VMEM) for _ in outs],
        out_shape=[jax.ShapeDtypeStruct(s, d) for s, d in outs],
        scratch_shapes=list(scratch),
        compiler_params=pltpu.CompilerParams(vmem_limit_bytes=20 * 1024 * 1024),
        cost_estimate=pl.CostEstimate(
            flops=int(us * 1.1e9), bytes_accessed=int(min(2 * moved, us * 3e6)), transcendentals=0
        ),
        name=name,
    )(*operands)


def bits_of(size):
    assert size & (size - 1) == 0
    return [size >> (k + 1) for k in range(size.bit_length() - 1)]


def across(value, bit):
    return lax.ppermute(value, "dp", [(i, i ^ bit) for i in range(lax.axis_size("dp"))])


def joined(arrays):
    return arrays[0] if len(arrays) == 1 else jnp.concatenate(arrays)


def widened(arrays, order, bit, step=across):
    whole = joined(arrays)
    return [whole, step(whole, bit)], order + [o ^ bit for o in order]


def halving_order(bits):
    order = [0]
    for bit in reversed(bits):
        order = order + [o ^ bit for o in order]
    return order


def swap(value, bit):
    return lax.ppermute(value, "tensor", [(t, t ^ bit) for t in range(lax.axis_size("tensor"))])


def gate(value, *earlier):
    return lax.optimization_barrier((value, *earlier))


class Held:
    def __init__(self, kept):
        self.kept = kept


class Halving(Held):
    def __init__(self, halves, steps):
        self.kept, self.sent = halves
        self.steps = list(steps)

    def step(self, *earlier):
        (move, bit), *self.steps = self.steps
        got, *kept = gate(move(self.sent, bit), *(e.kept for e in earlier))
        for e, k in zip(earlier, kept):
            e.kept = k
        if self.steps:
            half = self.kept.shape[0] // 2
            parts = [slice(None, half), slice(half, None)]
            self.kept, self.sent = (
                (self.kept[p].astype(F32) + got[p].astype(F32)).astype(BF16) for p in parts
            )
        else:
            self.kept, self.sent = self.kept[0].astype(F32) + got[0].astype(F32), None
        return self


def in_place(arrays, order, parts):
    if all(rows % 16 == 0 for rows in parts):
        return arrays, order, parts
    count = order.shape[0]
    stacked = joined(arrays)
    where = jnp.zeros((count,), jnp.int32).at[order].set(jnp.arange(count, dtype=jnp.int32))
    stacked = stacked[where]
    laid, at = [], 0
    for rows in parts:
        laid.append(stacked[:, at : at + rows].reshape(count * rows, -1))
        at += rows
    if at < stacked.shape[1]:
        laid.append(stacked[:, at:].astype(F32).sum(axis=0).astype(stacked.dtype))
    whole = jnp.concatenate(laid)[None]
    return [whole], jnp.zeros((1,), jnp.int32), [count * r for r in parts]


def norm_parts(rows):
    centred = rows - jnp.mean(rows, axis=-1, keepdims=True)
    rstd = lax.rsqrt(jnp.mean(centred * centred, axis=-1, keepdims=True) + EPSILON)
    return centred * rstd, rstd


def norm_pull(grad, gain, xhat, rstd):
    scaled = grad * gain
    level = jnp.mean(scaled, axis=-1, keepdims=True)
    along = jnp.mean(scaled * xhat, axis=-1, keepdims=True)
    return rstd * (scaled - level - xhat * along)


def colsum(rows):
    return jnp.sum(rows, axis=0, keepdims=True)


def each_piece(refs):
    k = 0
    for ref in refs:
        for j in range(ref.shape[0]):
            yield k, ref, j
            k += 1


def enter(seg, arrays, order, rows, seg_len, padded, width, cols):
    count = len(arrays)

    def kernel(order_ref, seg_ref, *refs):
        parts = refs[:count]
        w_out, xt_out, vec_out, x_scr = refs[count:]
        vec = 0.0
        for k, ref, j in each_piece(parts):
            start = pl.multiple_of(order_ref[k] * rows, 16)
            w_out[pl.ds(start, rows), :] = ref[j, 0:rows, :]
            vec = vec + ref[j, rows:, :].astype(F32)
        w_out[width:, :] = vec.astype(BF16)
        vec_out[...] = jnp.zeros(vec_out.shape, F32)
        for v in range(4):
            vec_out[v : v + 1, 0:cols] = vec[2 * v : 2 * v + 1, :]
            vec_out[v : v + 1, cols:width] = vec[2 * v + 1 : 2 * v + 2, 0 : width - cols]
        gain = vec_out[0:1, :]
        shift = vec_out[1:2, :]
        step = seg_len // 4

        def body(c, carry):
            at = pl.multiple_of(c * step, 16)
            xhat, _ = norm_parts(seg_ref[pl.ds(at, step), :].astype(F32))
            x_scr[pl.ds(at, step), :] = (xhat * gain + shift).astype(BF16)
            return carry

        lax.fori_loop(0, 4, body, 0)
        x_scr[seg_len:padded, :] = jnp.zeros((padded - seg_len, width), BF16)
        xt_out[...] = x_scr[...].T

    return call(
        kernel,
        (order, seg, *arrays),
        [((width + EXTRA, cols), BF16), ((width, padded), BF16), ((8, width), F32)],
        [pltpu.VMEM((padded, width), BF16)],
        scalars=1,
        name="enter",
        us=2.0,
    )


def lay_out(first, second, orders, parts, w, width):
    n_first, n_second = len(first), len(second)
    (out_rows, up_rows), (down_rows,) = parts
    cols = w.shape[1]
    counts = [sum(a.shape[0] for a in first), sum(a.shape[0] for a in second)]
    up_at = counts[0] * out_rows
    down_at = up_at + counts[0] * up_rows
    bias_at = down_at + counts[1] * down_rows

    def kernel(first_order, second_order, w_ref, *refs):
        wide = refs[-1]
        for k, ref, j in each_piece(refs[:n_first]):
            o = first_order[k]
            wide[pl.ds(pl.multiple_of(o * out_rows, 16), out_rows), :] = ref[j, 0:out_rows, :]
            start = pl.multiple_of(up_at + o * up_rows, 16)
            wide[pl.ds(start, up_rows), :] = ref[j, out_rows:, :]
        for k, ref, j in each_piece(refs[n_first : n_first + n_second]):
            start = pl.multiple_of(down_at + second_order[k] * down_rows, 16)
            wide[pl.ds(start, down_rows), :] = ref[j]
        bias = jnp.concatenate([w_ref[8:9, :], w_ref[9:10, 0 : width - cols]], axis=1)
        wide[bias_at:, :] = jnp.broadcast_to(bias, (EXTRA, width))

    return call(
        kernel,
        (*orders, w, *first, *second),
        [((bias_at + EXTRA, width), BF16)],
        scalars=2,
        name="lay_out",
        us=1.0,
        specs={2: pl.BlockSpec((EXTRA, cols), lambda i: (width // EXTRA, 0))},
    )[0]


def blocks_of(seg_len):
    return [(s, min(s + BLOCK, seg_len)) for s in range(0, seg_len, BLOCK)]


def one_head(block, h):
    row = lax.broadcasted_iota(jnp.int32, block.shape, 0)
    return jnp.where(row // HEAD == h, block, jnp.zeros_like(block))


def allowed_slots(live, start, stop):
    place = lax.broadcasted_iota(jnp.int32, (1, BLOCK), 1) + start
    bound = jnp.minimum(place, live - 1)
    return lax.broadcasted_iota(jnp.int32, (stop, BLOCK), 0) <= bound


def attend_forward(live, xt, w, cos, sin, seg_len):
    width, padded = xt.shape
    half = HEAD // 2

    def kernel(live_ref, xt_ref, w_ref, cos_ref, sin_ref, qkv_out, ot_out, mixed_out, lse_out):
        proj = nn(w_ref[0:width, :].T, xt_ref[...])
        cosine = cos_ref[...]
        sine = sin_ref[...]

        def rot(z):
            a, b = z[0:half], z[half:]
            return jnp.concatenate([a * cosine - b * sine, b * cosine + a * sine], axis=0)

        for h in range(2):
            r = h * HEAD
            qkv_out[r : r + HEAD, :] = (rot(proj[r : r + HEAD]) * HEAD ** (-0.5)).astype(BF16)
            r = r + PAIR
            qkv_out[r : r + HEAD, :] = rot(proj[r : r + HEAD]).astype(BF16)
        qkv_out[2 * PAIR :, :] = proj[2 * PAIR :].astype(BF16)
        keys = qkv_out[PAIR : 2 * PAIR, :].T
        lse_out[...] = jnp.zeros(lse_out.shape, F32)
        def head(h, carry):
            r = pl.multiple_of(h * HEAD, HEAD)
            for start, stop in blocks_of(seg_len):
                cols = slice(start, start + BLOCK)
                allowed = allowed_slots(live_ref[0], start, stop)
                query = one_head(qkv_out[0:PAIR, cols], h)
                scores = jnp.where(allowed, nn(keys[0:stop], query), MASKED)
                top = jnp.max(scores, axis=0, keepdims=True)
                weights = jnp.exp(scores - top)
                total = colsum(weights)
                probs = (weights * (1.0 / total)).astype(BF16)
                value = qkv_out[pl.ds(2 * PAIR + r, HEAD), 0:stop]
                ot_out[pl.ds(r, HEAD), cols] = nn(value, probs).astype(BF16)
                lse_out[pl.ds(h, 1), cols] = top + jnp.log(total)
            return carry

        lax.fori_loop(0, 2, head, 0)
        mixed_out[...] = ot_out[...].T[0:seg_len]

    return call(
        kernel,
        (live, xt, w, cos, sin),
        [
            ((3 * PAIR, padded), BF16),
            ((PAIR, padded), BF16),
            ((seg_len, PAIR), BF16),
            ((8, padded), F32),
        ],
        scalars=1,
        name="attend_forward",
        us=4.0,
    )


def emit(cut, order_ref, kept, sent):
    half = kept.shape[0]
    for k in range(2 * half):
        target, j = (kept, k) if k < half else (sent, k - half)
        cut(order_ref[k], target.at[j])


def attend_backward(live, xt, w, cos, sin, qkv, ot, lse, dot, acc, seg_len):
    width, padded = xt.shape
    half = HEAD // 2
    n_acc = len(acc)

    def kernel(live_ref, xt_ref, w_ref, cos_ref, sin_ref, qkv_ref, ot_ref, lse_ref, dot_ref, *refs):
        acc_refs = refs[:n_acc]
        acc_out, grad_out, d_scr, pg_scr, inner_scr = refs[n_acc:]
        cosine = cos_ref[...]
        sine = sin_ref[...]
        keys = qkv_ref[PAIR : 2 * PAIR, :].T
        values = qkv_ref[2 * PAIR :, :].T
        prod = dot_ref[...].astype(F32) * ot_ref[...].astype(F32)
        d_scr[...] = jnp.zeros(d_scr.shape, F32)
        for h in range(2):
            inner_scr[h : h + 1, :] = colsum(prod[h * HEAD : h * HEAD + HEAD])

        def head(h, carry):
            r = pl.multiple_of(h * HEAD, HEAD)
            q_at, k_at, v_at = (pl.ds(part * PAIR + r, HEAD) for part in range(3))
            for start, stop in blocks_of(seg_len):
                cols = slice(start, start + BLOCK)
                allowed = allowed_slots(live_ref[0], start, stop)
                query = one_head(qkv_ref[0:PAIR, cols], h)
                scores = jnp.where(allowed, nn(keys[0:stop], query), MASKED)
                probs = jnp.exp(scores - lse_ref[pl.ds(h, 1), cols])
                prob_grad = nn(values[0:stop], one_head(dot_ref[:, cols], h))
                score_grad = (probs * (prob_grad - inner_scr[pl.ds(h, 1), cols])).astype(BF16)
                d_scr[q_at, cols] = nn(qkv_ref[k_at, 0:stop], score_grad)
                d_scr[k_at, 0:stop] += nt(qkv_ref[q_at, cols], score_grad)
                d_scr[v_at, 0:stop] += nt(dot_ref[pl.ds(r, HEAD), cols], probs.astype(BF16))
            return carry

        lax.fori_loop(0, 2, head, 0)

        def unrot(z):
            a, b = z[0:half], z[half:]
            return jnp.concatenate([a * cosine + b * sine, b * cosine - a * sine], axis=0)

        for h in range(2):
            r = h * HEAD
            pg_scr[r : r + HEAD, :] = (unrot(d_scr[r : r + HEAD, :]) * HEAD ** (-0.5)).astype(BF16)
            r = r + PAIR
            pg_scr[r : r + HEAD, :] = unrot(d_scr[r : r + HEAD, :]).astype(BF16)
        pg_scr[2 * PAIR :, :] = d_scr[2 * PAIR :, :].astype(BF16)
        part = nn(w_ref[0:width, :], pg_scr[...])
        acc_out[...] = acc_refs[0][...] + part if n_acc else part
        grad_out[...] = nt(xt_ref[...], pg_scr[...]).astype(BF16)

    return call(
        kernel,
        (live, xt, w, cos, sin, qkv, ot, lse, dot, *acc),
        [((width, padded), F32), ((width, 3 * PAIR), BF16)],
        [
            pltpu.VMEM((3 * PAIR, padded), F32),
            pltpu.VMEM((3 * PAIR, padded), BF16),
            pltpu.VMEM((8, padded), F32),
        ],
        scalars=1,
        name="attend_backward",
        us=1.0,
    )


def rows_of(whole, first, index, rows):
    return whole[pl.ds(pl.multiple_of(first + index * rows, 16), rows), :]


def halves_call(kernel, operands, count, rows, cols, scratch, name):
    return call(
        kernel,
        operands,
        [((count // 2, rows, cols), BF16)] * 2,
        scratch,
        scalars=1,
        name=name,
        us=1.5,
    )


def packed(rows):
    n = rows.shape[0]
    tall = jnp.concatenate(jnp.split(rows, 3, axis=1))
    return jnp.concatenate(jnp.split(tall, 4), axis=1)


def unpacked(rows):
    tall = jnp.concatenate(jnp.split(rows, 4, axis=1))
    return jnp.stack(jnp.split(tall, 3), axis=1)


def cut_heads(grads, vec, outs, order, rows, out_rows):
    whole_rows, cols = grads[0].shape
    tall, width = outs[0].shape
    count = order.shape[0]
    unit = rows // 4
    high = 3 * unit

    def kernel(order_ref, a_ref, b_ref, c_ref, vec_ref, own_ref, near_ref, far_ref, kept, sent, whole, out_whole):
        whole[...] = (a_ref[...].astype(F32) + b_ref[...].astype(F32) + c_ref[...].astype(F32)).astype(BF16)
        out_sum = own_ref[...].astype(F32) + near_ref[0:tall, :].astype(F32) + far_ref[...].astype(F32)
        out_whole[...] = out_sum[0 : tall - EXTRA].astype(BF16)
        last = out_sum[tall - EXTRA :]
        last = jnp.concatenate([last[0:3], vec_ref[0:2, :], last[5:]], axis=0).astype(BF16)

        def cut(index, piece):
            for u in range(12):
                start = pl.multiple_of(index * rows + unit * (u % 4), 16)
                at, lane = unit * (u % 3), PAIR * (u // 3)
                block = whole[pl.ds(start, unit), PAIR * (u // 4) : PAIR * (u // 4 + 1)]
                piece[at : at + unit, lane : lane + PAIR] = block
            piece[high : high + out_rows, :] = rows_of(out_whole, 0, index, out_rows)
            piece[high + out_rows :, :] = last

        emit(cut, order_ref, kept, sent)

    return halves_call(
        kernel,
        (order, *grads, vec, *outs),
        count,
        high + out_rows + EXTRA,
        width,
        [pltpu.VMEM((whole_rows, cols), BF16), pltpu.VMEM((tall - EXTRA, width), BF16)],
        "cut_heads",
    )


def end_heads(kept, got, rows, out_rows):
    unit = rows // 4
    high = 3 * unit
    width = kept.shape[-1]

    def kernel(kept_ref, got_ref, qkv_out, out_out, vec_out):
        total = kept_ref[0].astype(F32) + got_ref[0].astype(F32)
        for u in range(12):
            at, lane = unit * (u % 3), PAIR * (u // 3)
            first = unit * (u % 4)
            qkv_out[first : first + unit, u // 4, :] = total[at : at + unit, lane : lane + PAIR]
        out_out[...] = total[high : high + out_rows]
        vec_out[...] = total[high + out_rows :]

    return call(
        kernel,
        (kept, got),
        [((rows, 3, PAIR), F32), ((out_rows, width), F32), ((EXTRA, width), F32)],
        name="end_heads",
        us=0.5,
    )


def cut_ffn(grads, up_order, down_order, rows):
    height, width = grads[0].shape
    count = up_order.shape[0]
    whole_rows = rows * count

    def kernel(up_ref, down_ref, a_ref, b_ref, c_ref, d_ref, up_kept, up_sent, down_kept, down_sent, near, far):
        half = up_kept.shape[0]
        for first, order_ref, kept, sent in (
            (0, up_ref, up_kept, up_sent),
            (whole_rows, down_ref, down_kept, down_sent),
        ):
            here = slice(first, first + whole_rows)
            near[...] = (a_ref[here, :].astype(F32) + b_ref[here, :].astype(F32)).astype(BF16)
            far[...] = (c_ref[here, :].astype(F32) + d_ref[here, :].astype(F32)).astype(BF16)
            for k in range(count):
                for side, whole in enumerate((near, far)):
                    j = 2 * k + side
                    target, j = (kept, j) if j < half else (sent, j - half)
                    target[j] = rows_of(whole, 0, order_ref[k], rows)

    outs = call(
        kernel,
        (up_order, down_order, *grads),
        [((count, rows, width), BF16)] * 4,
        [pltpu.VMEM((whole_rows, width), BF16)] * 2,
        scalars=2,
        name="cut_ffn",
        us=1.5,
    )
    return outs[0:2], outs[2:4]


def cut_thin(totals, order, spans, last=()):
    pieces = []
    for k in range(order.shape[0]):
        for total in totals:
            piece = [
                pack(lax.dynamic_slice_in_dim(total[part], order[k] * rows, rows, 0))
                for part, rows, pack in spans
            ]
            pieces.append(jnp.concatenate(piece + list(last)))
    pieces = jnp.stack(pieces)
    half = pieces.shape[0] // 2
    return pieces[:half], pieces[half:]


def added(arrays):
    return sum(a.astype(F32) for a in arrays).astype(BF16)


def merge_attention(seg, mixed, outs, vec):
    rows, width = seg.shape
    n = len(mixed)

    def kernel(seg_ref, vec_ref, *refs):
        mixed_refs, out_refs = refs[:n], refs[n : 2 * n]
        res_out, ffn_out = refs[2 * n :]
        gain = vec_ref[2:3, :]
        shift = vec_ref[3:4, :]
        step = rows // 2

        def body(c, carry):
            at = pl.multiple_of(c * step, 16)
            here = pl.ds(at, step)
            total = nn(mixed_refs[0][here, :], out_refs[0][...])
            for r in range(1, n):
                total = total + nn(mixed_refs[r][here, :], out_refs[r][...])
            total = total + seg_ref[here, :].astype(F32)
            res_out[here, :] = total
            xhat, _ = norm_parts(total)
            ffn_out[here, :] = (xhat * gain + shift).astype(BF16)
            return carry

        lax.fori_loop(0, 2, body, 0)

    return call(
        kernel,
        (seg, vec, *mixed, *outs),
        [((rows, width), F32), ((rows, width), BF16)],
        name="merge_attention",
        us=2.0,
        specs={2 + n + r: pl.BlockSpec((PAIR, width), lambda i: (0, 0)) for r in range(n)},
    )


def feed_forward(ffn_in, cot, wide, acc):
    rows, width = ffn_in.shape
    units = (wide.shape[0] - EXTRA - PAIR) // 2
    up_at, down_at, bias_at = PAIR, PAIR + units, PAIR + 2 * units
    n_acc = len(acc)

    def kernel(x_ref, cot_ref, ud_ref, *refs):
        acc_refs = refs[:n_acc]
        out_acc, back_acc, grad_out, act_scr, pg_scr = refs[n_acc:]
        step = rows // 2
        bias = ud_ref[bias_at : bias_at + 1, :].astype(F32)

        def body(c, total):
            at = pl.multiple_of(c * step, 16)
            here = pl.ds(at, step)
            up = ud_ref[up_at:down_at, :]
            down = ud_ref[down_at:bias_at, :]
            pre = nn(x_ref[here, :], up) + bias
            below = 0.5 + 0.5 * lax.erf(pre * 0.5**0.5)
            act = (pre * below).astype(BF16)
            slope = below + pre * (jnp.exp(-0.5 * (pre * pre)) * (1.0 / math.sqrt(2.0 * math.pi)))
            pre_grad = (nt(cot_ref[here, :], down) * slope).astype(BF16)
            act_scr[here, :] = act
            pg_scr[here, :] = pre_grad
            fwd = nn(act, down)
            back = nt(pre_grad, up)
            if n_acc:
                fwd = fwd + acc_refs[0][here, :]
                back = back + acc_refs[1][here, :]
            out_acc[here, :] = fwd
            back_acc[here, :] = back
            return total + colsum(pre_grad.astype(F32))

        total = lax.fori_loop(0, 2, body, jnp.zeros((1, units), F32))
        grad_out[0:units, :] = nn(x_ref[...].T, pg_scr[...]).astype(BF16)
        grad_out[units : 2 * units, :] = nn(act_scr[...].T, cot_ref[...]).astype(BF16)
        last = jnp.concatenate([total, jnp.zeros((EXTRA - 1, units), F32)], axis=0)
        grad_out[2 * units :, :] = last.astype(BF16)

    return call(
        kernel,
        (ffn_in, cot, wide, *acc),
        [((rows, width), F32), ((rows, width), F32), ((2 * units + EXTRA, width), BF16)],
        [pltpu.VMEM((rows, units), BF16), pltpu.VMEM((rows, units), BF16)],
        name="feed_forward",
        us=3.0,
    )


def turn_back(res, forward, backward, cot, vec, mixed_t, wides, ffn_grads, padded):
    rows, width = res.shape
    n = len(wides)
    out_rows = PAIR + EXTRA
    bias_at = ffn_grads[0].shape[0] // EXTRA - 1

    def kernel(res_ref, fwd_ref, back_ref, cot_ref, vec_ref, *refs):
        mixed_refs, out_refs, bias_refs = refs[:n], refs[n : 2 * n], refs[2 * n : 3 * n]
        block_out, resid_out, own_out, other_out, near_out = refs[3 * n : 3 * n + 5]
        dot_outs = refs[3 * n + 5 : 4 * n + 5]
        low_scr = refs[-1]
        gain = vec_ref[2:3, :]
        step = rows // 4

        def body(c, sums):
            here = pl.ds(pl.multiple_of(c * step, 16), step)
            res_rows = res_ref[here, :]
            back = back_ref[here, :]
            block_out[here, :] = (res_rows + fwd_ref[here, :]).astype(BF16)
            xhat, rstd = norm_parts(res_rows)
            resid = cot_ref[here, :].astype(F32) + norm_pull(back, gain, xhat, rstd)
            resid_out[here, :] = resid
            low_scr[here, :] = resid.astype(BF16)
            return sums[0] + colsum(back * xhat), sums[1] + colsum(back)

        zero = jnp.zeros((1, width), F32)
        gain_grad, shift_grad = lax.fori_loop(0, 4, body, (zero, zero))
        tail = jnp.zeros((EXTRA - 3, width), F32)
        low_scr[rows:, :] = jnp.zeros((padded - rows, width), BF16)
        places = [(own_out, 0), (near_out, 0), (other_out, 0), (near_out, out_rows)]
        for r, (target, at) in enumerate(places):
            dot_outs[r][...] = nt(out_refs[r][...], low_scr[...]).astype(BF16)
            grad = nn(mixed_refs[r][...], low_scr[...]).astype(BF16)
            target[at : at + PAIR, :] = grad
            last = [bias_refs[r][0:1, :].astype(F32), gain_grad, shift_grad, tail]
            target[at + PAIR : at + out_rows, :] = jnp.concatenate(last, axis=0).astype(BF16)

    return call(
        kernel,
        (res, forward, backward, cot, vec, *mixed_t, *wides, *ffn_grads),
        [((rows, width), BF16), ((rows, width), F32)]
        + [((out_rows, width), BF16)] * 2
        + [((2 * out_rows, width), BF16)]
        + [((PAIR, padded), BF16)] * n,
        [pltpu.VMEM((padded, width), BF16)],
        name="turn_back",
        us=0.5,
        specs={
            **{5 + n + r: pl.BlockSpec((PAIR, width), lambda i: (0, 0)) for r in range(n)},
            **{5 + 2 * n + r: pl.BlockSpec((EXTRA, width), lambda i: (bias_at, 0)) for r in range(n)},
        },
    )


def leave(seg, resid, acc, vec):
    rows, width = seg.shape
    padded = acc.shape[1]

    def kernel(seg_ref, resid_ref, acc_ref, vec_ref, seg_out, vec_out, acc_scr):
        gain = vec_ref[0:1, :]
        step = rows // 4
        acc_scr[...] = acc_ref[...].T

        def body(c, sums):
            here = pl.ds(pl.multiple_of(c * step, 16), step)
            grad = acc_scr[here, :]
            xhat, rstd = norm_parts(seg_ref[here, :].astype(F32))
            seg_out[here, :] = (resid_ref[here, :] + norm_pull(grad, gain, xhat, rstd)).astype(BF16)
            return sums[0] + colsum(grad * xhat), sums[1] + colsum(grad)

        zero = jnp.zeros((1, width), F32)
        gain_grad, shift_grad = lax.fori_loop(0, 4, body, (zero, zero))
        vec_out[...] = jnp.zeros(vec_out.shape, F32)
        vec_out[0:1, :] = gain_grad
        vec_out[1:2, :] = shift_grad

    return call(
        kernel,
        (seg, resid, acc, vec),
        [((rows, width), BF16), ((8, width), F32)],
        [pltpu.VMEM((padded, width), F32)],
        name="leave",
        us=0.5,
    )


def spread(mine, other, tensor_index, dtype):
    rows, width = mine.shape
    parts = [mine, swap(mine, 1), other, swap(other, 1)]

    def kernel(index_ref, *refs):
        out = refs[-1]
        for r, ref in enumerate(refs[:-1]):
            @pl.when(pl.program_id(0) == r)
            def _():
                out[0] = ref[...].astype(dtype)

    return pl.pallas_call(
        kernel,
        grid_spec=pltpu.PrefetchScalarGridSpec(
            num_scalar_prefetch=1,
            grid=(len(parts),),
            in_specs=[pl.BlockSpec((rows, width), lambda i, t: (0, 0)) for _ in parts],
            out_specs=pl.BlockSpec((1, rows, width), lambda i, t: (t[0] ^ i, 0, 0)),
        ),
        out_shape=jax.ShapeDtypeStruct((len(parts), rows, width), dtype),
        compiler_params=pltpu.CompilerParams(vmem_limit_bytes=24 * 1024 * 1024),
        name="spread",
    )(jnp.reshape(tensor_index, (1,)).astype(jnp.int32), *parts)


def own_shares(norm_vecs, ffn_vecs, place, share):
    width = ffn_vecs.shape[1]

    def kernel(place_ref, norm_ref, ffn_ref, *outs):
        whole = jnp.concatenate([norm_ref[3:5, :], ffn_ref[0:3, :]], axis=0)
        total = jnp.zeros((whole.shape[0], share), F32)
        for k in range(width // share):
            part = whole[:, k * share : (k + 1) * share]
            total = total + jnp.where(place_ref[0] == k, part, jnp.zeros_like(part))
        for v, out in enumerate(outs):
            out[...] = total[v : v + 1]

    outs = call(
        kernel,
        (jnp.reshape(place, (1,)).astype(jnp.int32), norm_vecs, ffn_vecs),
        [((1, share), F32)] * 5,
        scalars=1,
        name="own_shares",
    )
    return [o.reshape(share) for o in outs]


def rotary_tables(starts, padded):
    half = HEAD // 2
    inverse = jnp.exp(jnp.arange(half).astype(F32) * (-math.log(10000.0) / half))
    angles = inverse[:, None] * starts.astype(F32)[None, :]
    angles = jnp.pad(angles, ((0, 0), (0, padded - starts.shape[0])))
    return jnp.cos(angles), jnp.sin(angles)


def vector_rows(vectors, here, width, cols):
    own = vectors[0].shape[0]
    stacked = jnp.stack(vectors + (jnp.zeros_like(vectors[0]),) * (8 - len(vectors)))
    lanes = -(-cols // own) * own

    def kernel(here_ref, vec_ref, out):
        tiled = jnp.concatenate([vec_ref[...].astype(F32)] * (lanes // own), axis=1)[:, 0:cols]
        place = lax.broadcasted_iota(jnp.int32, tiled.shape, 1)
        first = here_ref[0] * own
        rows = []
        for v in range(len(vectors)):
            for at in (0, cols):
                inside = (place + at >= first) & (place + at < first + own)
                rows.append(jnp.where(inside, tiled, 0.0)[v : v + 1])
        rows.append(jnp.zeros((EXTRA - len(rows), cols), F32))
        out[...] = jnp.concatenate(rows, axis=0).astype(BF16)

    return call(
        kernel,
        (jnp.reshape(here, (1,)).astype(jnp.int32), stacked),
        [((EXTRA, cols), BF16)],
        scalars=1,
        name="vector_rows",
        us=0.3,
    )[0]


def local(
    segments,
    seg_start,
    seg_count,
    norm_gain,
    norm_shift,
    qkv_weight,
    out_weight,
    ffn_gain,
    ffn_shift,
    up_weight,
    up_bias,
    down_weight,
    cotangent,
):
    seq_local, seg_len, width = segments.shape
    tensor = lax.axis_size("tensor")
    members = lax.axis_size("dp")
    assert seq_local == tensor == 4
    padded = -(-seg_len // BLOCK) * BLOCK
    bits = bits_of(members)
    here = lax.axis_index("dp")
    mine = lax.axis_index("tensor")
    cols = 3 * qkv_weight.shape[2]
    assert cols == 3 * PAIR and width * 2 > cols
    groups = range(tensor)
    thin = any(
        a.shape[0] % 16 for a in (qkv_weight, out_weight, up_weight, down_weight)
    )

    seg = lax.dynamic_index_in_dim(segments, mine, 0, keepdims=False)
    cot = lax.dynamic_index_in_dim(cotangent, mine, 0, keepdims=False)
    starts = lax.dynamic_index_in_dim(seg_start, mine, 0, keepdims=False)
    live = lax.dynamic_slice_in_dim(seg_count, mine, 1)
    cos, sin = rotary_tables(starts, padded)

    def indices(distances):
        return here ^ jnp.asarray(distances, jnp.int32)

    qkv_rows, out_rows = qkv_weight.shape[0], out_weight.shape[0]
    up_rows, down_rows = up_weight.shape[0], down_weight.shape[0]
    vectors = (norm_gain, norm_shift, ffn_gain, ffn_shift, up_bias)
    first = jnp.concatenate(
        [qkv_weight.reshape(-1, cols), vector_rows(vectors, here, width, cols)]
    )
    arrays, order = [first[None]], [0]
    side, side_order = [jnp.concatenate([out_weight, up_weight])[None]], [0]
    down, down_order = [down_weight[None]], [0]
    for bit in bits[:-1]:
        arrays, order = widened(arrays, order, bit)
        side, side_order = widened(side, side_order, bit)
        down, down_order = widened(down, down_order, bit)
    arrays, order = widened(arrays, order, bits[-1])
    side, side_order = widened(side, side_order, bits[-1])
    down = joined(down)
    down = [down, swap(down, 2)]
    down_far = [across(d, bits[-1]) for d in down]
    down_order = down_order + [o ^ bits[-1] for o in down_order]

    pieces, places, parts = in_place(arrays, indices(order), (qkv_rows,))
    w0, xt, vec = enter(seg, pieces, places, parts[0], seg_len, padded, width, cols)
    def weights_of(side, down, w):
        s, s_places, s_parts = in_place(side, indices(side_order), (out_rows, up_rows))
        d, d_places, d_parts = in_place(down, indices(down_order), (down_rows,))
        return lay_out(s, d, (s_places, d_places), (s_parts, d_parts), w, width)

    def attend(w):
        return list(attend_forward(live, xt, w, cos, sin, seg_len))

    w = [w0, swap(w0, 1), swap(w0, 2), None]
    far = [swap(s, 2) for s in side]
    heads = [attend(w[0])]
    w[1], heads[0][2] = gate(w[1], heads[0][2])
    heads.append(attend(w[1]))
    *near, heads[1][2] = gate(*side, down[0], down_far[0], heads[1][2])
    wides = [weights_of(near[:-2], near[-2:], w0)]
    wides.append(swap(wides[0], 1))
    w[2], wides[0] = gate(w[2], wides[0])
    w[3] = swap(w[2], 1)
    heads.append(attend(w[2]))
    w[3], heads[2][2] = gate(w[3], heads[2][2])
    heads.append(attend(w[3]))
    *far, heads[3][2] = gate(*far, down[1], down_far[1], heads[3][2])
    wides.append(weights_of(far[:-2], far[-2:], w[2]))
    wides.append(swap(wides[2], 1))
    res, ffn_in = merge_attention(seg, [h[2] for h in heads], wides, vec)
    up_bits, down_bits = bits[::-1], bits[-2::-1] + bits[-1:]
    ahead, down_ahead = (indices(halving_order(b)) for b in (up_bits, down_bits))
    acc = ()
    ffn_grads = [None] * 4
    for r in (3, 2, 1, 0):
        out_acc, back_acc, ffn_grads[r] = feed_forward(ffn_in, cot, wides[r], acc)
        acc = (out_acc, back_acc)
    ups = (ffn_grads[0], swap(ffn_grads[1], 1), ffn_grads[2], swap(ffn_grads[3], 1))
    units = (ffn_grads[0].shape[0] - EXTRA) // 2
    if thin:
        pairs = [added(ups[0:2]), added(ups[2:4])]
        keep = lambda rows: rows
        up_halves = cut_thin([[p[:units]] for p in pairs], ahead, [(0, up_rows, keep)])
        down_halves = cut_thin(
            [[p[units : 2 * units]] for p in pairs], down_ahead, [(0, down_rows, keep)]
        )
    else:
        up_halves, down_halves = cut_ffn(ups, ahead, down_ahead, up_rows)
    res, up_halves, down_halves = lax.optimization_barrier((res, up_halves, down_halves))
    up = Halving(up_halves, [(across, b) for b in up_bits] + [(swap, 2)])
    down = Halving(down_halves, [(across, b) for b in down_bits] + [(swap, 2)])
    turned = turn_back(
        res, *acc, cot, vec, [h[1] for h in heads], wides, ffn_grads, padded
    )
    block_mine, resid, out_own, out_other, out_near = turned[0:5]
    dots = list(turned[5:9])
    block_out = spread(block_mine, swap(block_mine, 2), mine, BF16)
    out_near = swap(out_near, 1)
    out_far = swap(added([out_other, out_near[out_other.shape[0] :]]), 2)

    acc = ()
    qkv_grads = [None] * 4
    for r in (3, 2, 1, 0):
        if r == 2:
            up.step()
            down.step()
            dots[r], up.kept, up.sent, down.kept, down.sent = gate(
                dots[r], up.kept, up.sent, down.kept, down.sent
            )
        if r == 1:
            dots[r], other, out_far = gate(dots[r], other, out_far)
        qkv, ot, _, lse = heads[r]
        total, qkv_grads[r] = attend_backward(
            live, xt, w[r], cos, sin, qkv, ot, lse, dots[r], acc, seg_len
        )
        acc = (total,)
        if r == 2:
            other = added([qkv_grads[2], swap(qkv_grads[3], 1)])
    up.step()
    down.step()
    total, up.kept, up.sent, down.kept, down.sent = gate(
        total, up.kept, up.sent, down.kept, down.sent
    )
    seg_mine, norm_vec = leave(seg, resid, total, vec)
    seg_mine = Held(seg_mine)
    seg_other = Held(swap(seg_mine.kept, 2))
    other, seg_mine.kept = gate(swap(other, 2), seg_mine.kept)
    parts = (qkv_grads[0], swap(qkv_grads[1], 1), other)
    if thin:
        tall = out_own.shape[0]
        out_sum = added([out_own, out_near[:tall], out_far])
        last = out_sum[-EXTRA:].at[3:5].set(norm_vec[0:2].astype(BF16))
        halves = cut_thin(
            [[added(parts), out_sum]], ahead, [(0, qkv_rows, packed), (1, out_rows, keep)], [last]
        )
    else:
        halves = cut_heads(parts, norm_vec, (out_own, out_near, out_far), ahead, qkv_rows, out_rows)
    heads_sum = Halving(halves, [(across, b) for b in up_bits])
    down.step(heads_sum)
    block_out, down.kept = gate(block_out, down.kept)
    up.step(down)
    heads_sum.step(up)
    while len(heads_sum.steps) > 1:
        heads_sum.step()
    seg_other.kept, heads_sum.kept, heads_sum.sent = gate(
        seg_other.kept, heads_sum.kept, heads_sum.sent
    )
    while up.steps:
        up.step(seg_other)
        down.step(up)
    up_g, down_g = up.kept, down.kept
    got = across(heads_sum.sent, heads_sum.steps[0][1])
    got, up_g, down_g = gate(got, up_g, down_g)
    if thin:
        total = heads_sum.kept[0].astype(F32) + got[0].astype(F32)
        high = 3 * qkv_rows // 4
        qkv_g = unpacked(total[:high])
        out_g, vecs = total[high : high + out_rows], total[high + out_rows :]
    else:
        qkv_g, out_g, vecs = end_heads(heads_sum.kept, got, qkv_rows, out_rows)
    near_vecs = vecs + swap(vecs, 1)
    near_vecs, seg_mine.kept = gate(near_vecs, seg_mine.kept)
    segments_grad = spread(seg_mine.kept, seg_other.kept, mine, F32)
    far_vecs, segments_grad = gate(swap(near_vecs, 2), segments_grad)
    norm_vecs = near_vecs + far_vecs

    share = norm_gain.shape[0]
    assert cols % share == 0
    assert up_bias.shape[0] == share
    norm_gain_g, norm_shift_g, bias_g, ffn_gain_g, ffn_shift_g = own_shares(
        norm_vecs, vecs, here, share
    )
    return (
        block_out,
        segments_grad,
        norm_gain_g,
        norm_shift_g,
        qkv_g,
        out_g,
        ffn_gain_g,
        ffn_shift_g,
        up_g,
        bias_g,
        down_g,
    )


def solution(mesh):
    placed = (
        P("dp", None, None),
        P("dp", None),
        P("dp"),
        P("dp"),
        P("dp"),
        P("dp", None, "tensor"),
        P(("tensor", "dp"), None),
        P("dp"),
        P("dp"),
        P("dp", "tensor"),
        P(("tensor", "dp")),
        P(("tensor", "dp"), None),
        P("dp", None, None),
    )
    return jax.shard_map(
        local,
        mesh=mesh,
        in_specs=placed,
        out_specs=(
            P("dp", None, None),
            P("dp", None, None),
            P("dp"),
            P("dp"),
            P("dp", None, "tensor"),
            P(("tensor", "dp"), None),
            P("dp"),
            P("dp"),
            P("dp", "tensor"),
            P(("tensor", "dp")),
            P(("tensor", "dp"), None),
        ),
        check_vma=False,
    )
```

```python
import math

import jax
import jax.numpy as jnp
from jax import lax
from jax.experimental import pallas as pl
from jax.experimental.pallas import tpu as pltpu
from jax.sharding import PartitionSpec as P

HEAD = 64
PAIR = 2 * HEAD
BLOCK = 256
EPSILON = 1e-05
MASKED = -1e30
BF16 = jnp.bfloat16
F32 = jnp.float32
EXTRA = 16


def nn(a, b):
    return lax.dot_general(a, b, (((1,), (0,)), ((), ())), preferred_element_type=F32)


def nt(a, b):
    return lax.dot_general(a, b, (((1,), (1,)), ((), ())), preferred_element_type=F32)


def call(kernel, operands, outs, scratch=(), scalars=0, name=None, us=1.0, specs=None):
    inner = [pl.BlockSpec(memory_space=pltpu.SMEM) for _ in range(scalars)]
    inner += [pl.BlockSpec(memory_space=pltpu.VMEM) for _ in operands[scalars:]]
    for at, spec in (specs or {}).items():
        inner[at] = spec
    moved = sum(math.prod(s) * jnp.dtype(d).itemsize for s, d in outs)
    return pl.pallas_call(
        kernel,
        grid=(1,),
        in_specs=inner,
        out_specs=[pl.BlockSpec(memory_space=pltpu.VMEM) for _ in outs],
        out_shape=[jax.ShapeDtypeStruct(s, d) for s, d in outs],
        scratch_shapes=list(scratch),
        compiler_params=pltpu.CompilerParams(vmem_limit_bytes=20 * 1024 * 1024),
        cost_estimate=pl.CostEstimate(
            flops=int(us * 1.1e9), bytes_accessed=int(min(2 * moved, us * 3e6)), transcendentals=0
        ),
        name=name,
    )(*operands)


def bits_of(size):
    assert size & (size - 1) == 0
    return [size >> (k + 1) for k in range(size.bit_length() - 1)]


def across(value, bit):
    return lax.ppermute(value, "dp", [(i, i ^ bit) for i in range(lax.axis_size("dp"))])


def joined(arrays):
    return arrays[0] if len(arrays) == 1 else jnp.concatenate(arrays)


def widened(arrays, order, bit, step=across):
    whole = joined(arrays)
    return [whole, step(whole, bit)], order + [o ^ bit for o in order]


def halving_order(bits):
    order = [0]
    for bit in reversed(bits):
        order = order + [o ^ bit for o in order]
    return order


def swap(value, bit):
    return lax.ppermute(value, "tensor", [(t, t ^ bit) for t in range(lax.axis_size("tensor"))])


def gate(value, *earlier):
    return lax.optimization_barrier((value, *earlier))


class Held:
    def __init__(self, kept):
        self.kept = kept


class Halving(Held):
    def __init__(self, halves, steps):
        self.kept, self.sent = halves
        self.steps = list(steps)

    def step(self, *earlier):
        (move, bit), *self.steps = self.steps
        got, *kept = gate(move(self.sent, bit), *(e.kept for e in earlier))
        for e, k in zip(earlier, kept):
            e.kept = k
        if self.kept.shape[0] > 1:
            half = self.kept.shape[0] // 2
            parts = [slice(None, half), slice(half, None)]
            self.kept, self.sent = (
                (self.kept[p].astype(F32) + got[p].astype(F32)).astype(BF16) for p in parts
            )
        else:
            self.kept, self.sent = self.kept[0].astype(F32) + got[0].astype(F32), None
        return self


def in_place(arrays, order, parts):
    if all(rows % 16 == 0 for rows in parts):
        return arrays, order, parts
    count = order.shape[0]
    stacked = joined(arrays)
    where = jnp.zeros((count,), jnp.int32).at[order].set(jnp.arange(count, dtype=jnp.int32))
    stacked = stacked[where]
    laid, at = [], 0
    for rows in parts:
        laid.append(stacked[:, at : at + rows].reshape(count * rows, -1))
        at += rows
    if at < stacked.shape[1]:
        laid.append(stacked[:, at:].astype(F32).sum(axis=0).astype(stacked.dtype))
    whole = jnp.concatenate(laid)[None]
    return [whole], jnp.zeros((1,), jnp.int32), [count * r for r in parts]


def norm_parts(rows):
    centred = rows - jnp.mean(rows, axis=-1, keepdims=True)
    rstd = lax.rsqrt(jnp.mean(centred * centred, axis=-1, keepdims=True) + EPSILON)
    return centred * rstd, rstd


def norm_pull(grad, gain, xhat, rstd):
    scaled = grad * gain
    level = jnp.mean(scaled, axis=-1, keepdims=True)
    along = jnp.mean(scaled * xhat, axis=-1, keepdims=True)
    return rstd * (scaled - level - xhat * along)


def colsum(rows):
    return jnp.sum(rows, axis=0, keepdims=True)


def each_piece(refs):
    k = 0
    for ref in refs:
        for j in range(ref.shape[0]):
            yield k, ref, j
            k += 1


def enter(seg, arrays, order, rows, seg_len, padded, width, cols):
    count = len(arrays)

    def kernel(order_ref, seg_ref, *refs):
        parts = refs[:count]
        w_out, xt_out, vec_out, x_scr = refs[count:]
        vec = 0.0
        for k, ref, j in each_piece(parts):
            start = pl.multiple_of(order_ref[k] * rows, 16)
            w_out[pl.ds(start, rows), :] = ref[j, 0:rows, :]
            vec = vec + ref[j, rows:, :].astype(F32)
        w_out[width:, :] = vec.astype(BF16)
        vec_out[...] = jnp.zeros(vec_out.shape, F32)
        for v in range(4):
            vec_out[v : v + 1, 0:cols] = vec[2 * v : 2 * v + 1, :]
            vec_out[v : v + 1, cols:width] = vec[2 * v + 1 : 2 * v + 2, 0 : width - cols]
        gain = vec_out[0:1, :]
        shift = vec_out[1:2, :]
        step = seg_len // 4

        def body(c, carry):
            at = pl.multiple_of(c * step, 16)
            xhat, _ = norm_parts(seg_ref[pl.ds(at, step), :].astype(F32))
            x_scr[pl.ds(at, step), :] = (xhat * gain + shift).astype(BF16)
            return carry

        lax.fori_loop(0, 4, body, 0)
        x_scr[seg_len:padded, :] = jnp.zeros((padded - seg_len, width), BF16)
        xt_out[...] = x_scr[...].T

    return call(
        kernel,
        (order, seg, *arrays),
        [((width + EXTRA, cols), BF16), ((width, padded), BF16), ((8, width), F32)],
        [pltpu.VMEM((padded, width), BF16)],
        scalars=1,
        name="enter",
        us=2.0,
    )


def lay_out(first, second, orders, parts, w, width):
    n_first, n_second = len(first), len(second)
    (out_rows, up_rows), (down_rows,) = parts
    cols = w.shape[1]
    counts = [sum(a.shape[0] for a in first), sum(a.shape[0] for a in second)]
    up_at = counts[0] * out_rows
    down_at = up_at + counts[0] * up_rows
    bias_at = down_at + counts[1] * down_rows

    def kernel(first_order, second_order, w_ref, *refs):
        wide = refs[-1]
        for k, ref, j in each_piece(refs[:n_first]):
            o = first_order[k]
            wide[pl.ds(pl.multiple_of(o * out_rows, 16), out_rows), :] = ref[j, 0:out_rows, :]
            start = pl.multiple_of(up_at + o * up_rows, 16)
            wide[pl.ds(start, up_rows), :] = ref[j, out_rows:, :]
        for k, ref, j in each_piece(refs[n_first : n_first + n_second]):
            start = pl.multiple_of(down_at + second_order[k] * down_rows, 16)
            wide[pl.ds(start, down_rows), :] = ref[j]
        bias = jnp.concatenate([w_ref[8:9, :], w_ref[9:10, 0 : width - cols]], axis=1)
        wide[bias_at:, :] = jnp.broadcast_to(bias, (EXTRA, width))

    return call(
        kernel,
        (*orders, w, *first, *second),
        [((bias_at + EXTRA, width), BF16)],
        scalars=2,
        name="lay_out",
        us=1.0,
        specs={2: pl.BlockSpec((EXTRA, cols), lambda i: (width // EXTRA, 0))},
    )[0]


def blocks_of(seg_len):
    return [(s, min(s + BLOCK, seg_len)) for s in range(0, seg_len, BLOCK)]


def one_head(block, h):
    row = lax.broadcasted_iota(jnp.int32, block.shape, 0)
    return jnp.where(row // HEAD == h, block, jnp.zeros_like(block))


def allowed_slots(live, start, stop):
    place = lax.broadcasted_iota(jnp.int32, (1, BLOCK), 1) + start
    bound = jnp.minimum(place, live - 1)
    return lax.broadcasted_iota(jnp.int32, (stop, BLOCK), 0) <= bound


def attend_forward(live, xt, w, cos, sin, seg_len):
    width, padded = xt.shape
    half = HEAD // 2

    def kernel(live_ref, xt_ref, w_ref, cos_ref, sin_ref, qkv_out, ot_out, mixed_out, lse_out):
        proj = nn(w_ref[0:width, :].T, xt_ref[...])
        cosine = cos_ref[...]
        sine = sin_ref[...]

        def rot(z):
            a, b = z[0:half], z[half:]
            return jnp.concatenate([a * cosine - b * sine, b * cosine + a * sine], axis=0)

        for h in range(2):
            r = h * HEAD
            qkv_out[r : r + HEAD, :] = (rot(proj[r : r + HEAD]) * HEAD ** (-0.5)).astype(BF16)
            r = r + PAIR
            qkv_out[r : r + HEAD, :] = rot(proj[r : r + HEAD]).astype(BF16)
        qkv_out[2 * PAIR :, :] = proj[2 * PAIR :].astype(BF16)
        keys = qkv_out[PAIR : 2 * PAIR, :].T
        lse_out[...] = jnp.zeros(lse_out.shape, F32)
        def head(h, carry):
            r = pl.multiple_of(h * HEAD, HEAD)
            for start, stop in blocks_of(seg_len):
                cols = slice(start, start + BLOCK)
                allowed = allowed_slots(live_ref[0], start, stop)
                query = one_head(qkv_out[0:PAIR, cols], h)
                scores = jnp.where(allowed, nn(keys[0:stop], query), MASKED)
                top = jnp.max(scores, axis=0, keepdims=True)
                weights = jnp.exp(scores - top)
                total = colsum(weights)
                probs = (weights * (1.0 / total)).astype(BF16)
                value = qkv_out[pl.ds(2 * PAIR + r, HEAD), 0:stop]
                ot_out[pl.ds(r, HEAD), cols] = nn(value, probs).astype(BF16)
                lse_out[pl.ds(h, 1), cols] = top + jnp.log(total)
            return carry

        lax.fori_loop(0, 2, head, 0)
        mixed_out[...] = ot_out[...].T[0:seg_len]

    return call(
        kernel,
        (live, xt, w, cos, sin),
        [
            ((3 * PAIR, padded), BF16),
            ((PAIR, padded), BF16),
            ((seg_len, PAIR), BF16),
            ((8, padded), F32),
        ],
        scalars=1,
        name="attend_forward",
        us=4.0,
    )


def emit(cut, order_ref, kept, sent):
    half = kept.shape[0]
    for k in range(2 * half):
        target, j = (kept, k) if k < half else (sent, k - half)
        cut(order_ref[k], target.at[j])


def attend_backward(live, xt, w, cos, sin, qkv, ot, lse, dot, acc, seg_len):
    width, padded = xt.shape
    half = HEAD // 2
    n_acc = len(acc)

    def kernel(live_ref, xt_ref, w_ref, cos_ref, sin_ref, qkv_ref, ot_ref, lse_ref, dot_ref, *refs):
        acc_refs = refs[:n_acc]
        acc_out, grad_out, d_scr, pg_scr, inner_scr = refs[n_acc:]
        cosine = cos_ref[...]
        sine = sin_ref[...]
        keys = qkv_ref[PAIR : 2 * PAIR, :].T
        values = qkv_ref[2 * PAIR :, :].T
        prod = dot_ref[...].astype(F32) * ot_ref[...].astype(F32)
        d_scr[...] = jnp.zeros(d_scr.shape, F32)
        for h in range(2):
            inner_scr[h : h + 1, :] = colsum(prod[h * HEAD : h * HEAD + HEAD])

        def head(h, carry):
            r = pl.multiple_of(h * HEAD, HEAD)
            q_at, k_at, v_at = (pl.ds(part * PAIR + r, HEAD) for part in range(3))
            for start, stop in blocks_of(seg_len):
                cols = slice(start, start + BLOCK)
                allowed = allowed_slots(live_ref[0], start, stop)
                query = one_head(qkv_ref[0:PAIR, cols], h)
                scores = jnp.where(allowed, nn(keys[0:stop], query), MASKED)
                probs = jnp.exp(scores - lse_ref[pl.ds(h, 1), cols])
                prob_grad = nn(values[0:stop], one_head(dot_ref[:, cols], h))
                score_grad = (probs * (prob_grad - inner_scr[pl.ds(h, 1), cols])).astype(BF16)
                d_scr[q_at, cols] = nn(qkv_ref[k_at, 0:stop], score_grad)
                d_scr[k_at, 0:stop] += nt(qkv_ref[q_at, cols], score_grad)
                d_scr[v_at, 0:stop] += nt(dot_ref[pl.ds(r, HEAD), cols], probs.astype(BF16))
            return carry

        lax.fori_loop(0, 2, head, 0)

        def unrot(z):
            a, b = z[0:half], z[half:]
            return jnp.concatenate([a * cosine + b * sine, b * cosine - a * sine], axis=0)

        for h in range(2):
            r = h * HEAD
            pg_scr[r : r + HEAD, :] = (unrot(d_scr[r : r + HEAD, :]) * HEAD ** (-0.5)).astype(BF16)
            r = r + PAIR
            pg_scr[r : r + HEAD, :] = unrot(d_scr[r : r + HEAD, :]).astype(BF16)
        pg_scr[2 * PAIR :, :] = d_scr[2 * PAIR :, :].astype(BF16)
        part = nn(w_ref[0:width, :], pg_scr[...])
        acc_out[...] = acc_refs[0][...] + part if n_acc else part
        grad_out[...] = nt(xt_ref[...], pg_scr[...]).astype(BF16)

    return call(
        kernel,
        (live, xt, w, cos, sin, qkv, ot, lse, dot, *acc),
        [((width, padded), F32), ((width, 3 * PAIR), BF16)],
        [
            pltpu.VMEM((3 * PAIR, padded), F32),
            pltpu.VMEM((3 * PAIR, padded), BF16),
            pltpu.VMEM((8, padded), F32),
        ],
        scalars=1,
        name="attend_backward",
        us=1.0,
    )


def rows_of(whole, first, index, rows):
    return whole[pl.ds(pl.multiple_of(first + index * rows, 16), rows), :]


def halves_call(kernel, operands, count, rows, cols, scratch, name):
    return call(
        kernel,
        operands,
        [((count // 2, rows, cols), BF16)] * 2,
        scratch,
        scalars=1,
        name=name,
        us=1.5,
    )


def packed(rows):
    n = rows.shape[0]
    tall = jnp.concatenate(jnp.split(rows, 3, axis=1))
    return jnp.concatenate(jnp.split(tall, 4), axis=1)


def unpacked(rows):
    tall = jnp.concatenate(jnp.split(rows, 4, axis=1))
    return jnp.stack(jnp.split(tall, 3), axis=1)


def cut_heads(grads, vec, outs, order, rows, out_rows):
    whole_rows, cols = grads[0].shape
    tall, width = outs[0].shape
    count = order.shape[0]
    unit = rows // 4
    high = 3 * unit

    def kernel(order_ref, a_ref, b_ref, c_ref, vec_ref, own_ref, near_ref, far_ref, kept, sent, whole, out_whole):
        whole[...] = (a_ref[...].astype(F32) + b_ref[...].astype(F32) + c_ref[...].astype(F32)).astype(BF16)
        out_sum = own_ref[...].astype(F32) + near_ref[0:tall, :].astype(F32) + far_ref[...].astype(F32)
        out_whole[...] = out_sum[0 : tall - EXTRA].astype(BF16)
        last = out_sum[tall - EXTRA :]
        last = jnp.concatenate([last[0:3], vec_ref[0:2, :], last[5:]], axis=0).astype(BF16)

        def cut(index, piece):
            for u in range(12):
                start = pl.multiple_of(index * rows + unit * (u % 4), 16)
                at, lane = unit * (u % 3), PAIR * (u // 3)
                block = whole[pl.ds(start, unit), PAIR * (u // 4) : PAIR * (u // 4 + 1)]
                piece[at : at + unit, lane : lane + PAIR] = block
            piece[high : high + out_rows, :] = rows_of(out_whole, 0, index, out_rows)
            piece[high + out_rows :, :] = last

        emit(cut, order_ref, kept, sent)

    return halves_call(
        kernel,
        (order, *grads, vec, *outs),
        count,
        high + out_rows + EXTRA,
        width,
        [pltpu.VMEM((whole_rows, cols), BF16), pltpu.VMEM((tall - EXTRA, width), BF16)],
        "cut_heads",
    )


def end_heads(kept, got, rows, out_rows):
    unit = rows // 4
    high = 3 * unit
    width = kept.shape[-1]

    def kernel(kept_ref, got_ref, qkv_out, out_out, vec_out):
        total = kept_ref[0].astype(F32) + got_ref[0].astype(F32)
        for u in range(12):
            at, lane = unit * (u % 3), PAIR * (u // 3)
            first = unit * (u % 4)
            qkv_out[first : first + unit, u // 4, :] = total[at : at + unit, lane : lane + PAIR]
        out_out[...] = total[high : high + out_rows]
        vec_out[...] = total[high + out_rows :]

    return call(
        kernel,
        (kept, got),
        [((rows, 3, PAIR), F32), ((out_rows, width), F32), ((EXTRA, width), F32)],
        name="end_heads",
        us=0.5,
    )


def end_ffn(up_kept, down_kept, got):
    def kernel(up_ref, down_ref, got_ref, up_out, down_out):
        up_out[...] = up_ref[0].astype(F32) + got_ref[0].astype(F32)
        down_out[...] = down_ref[0].astype(F32) + got_ref[1].astype(F32)

    return call(
        kernel,
        (up_kept, down_kept, got),
        [(up_kept.shape[1:], F32), (down_kept.shape[1:], F32)],
        name="end_ffn",
        us=0.3,
    )


def cut_ffn(grads, up_order, down_order, rows):
    height, width = grads[0].shape
    count = up_order.shape[0]
    whole_rows = rows * count

    def kernel(up_ref, down_ref, a_ref, b_ref, c_ref, d_ref, up_kept, up_sent, down_kept, down_sent, near, far):
        half = up_kept.shape[0]
        for first, order_ref, kept, sent in (
            (0, up_ref, up_kept, up_sent),
            (whole_rows, down_ref, down_kept, down_sent),
        ):
            here = slice(first, first + whole_rows)
            near[...] = (a_ref[here, :].astype(F32) + b_ref[here, :].astype(F32)).astype(BF16)
            far[...] = (c_ref[here, :].astype(F32) + d_ref[here, :].astype(F32)).astype(BF16)
            for k in range(count):
                for side, whole in enumerate((near, far)):
                    j = 2 * k + side
                    target, j = (kept, j) if j < half else (sent, j - half)
                    target[j] = rows_of(whole, 0, order_ref[k], rows)

    outs = call(
        kernel,
        (up_order, down_order, *grads),
        [((count, rows, width), BF16)] * 4,
        [pltpu.VMEM((whole_rows, width), BF16)] * 2,
        scalars=2,
        name="cut_ffn",
        us=1.5,
    )
    return outs[0:2], outs[2:4]


def cut_thin(totals, order, spans, last=()):
    pieces = []
    for k in range(order.shape[0]):
        for total in totals:
            piece = [
                pack(lax.dynamic_slice_in_dim(total[part], order[k] * rows, rows, 0))
                for part, rows, pack in spans
            ]
            pieces.append(jnp.concatenate(piece + list(last)))
    pieces = jnp.stack(pieces)
    half = pieces.shape[0] // 2
    return pieces[:half], pieces[half:]


def added(arrays):
    return sum(a.astype(F32) for a in arrays).astype(BF16)


def merge_attention(seg, mixed, outs, vec):
    rows, width = seg.shape
    n = len(mixed)

    def kernel(seg_ref, vec_ref, *refs):
        mixed_refs, out_refs = refs[:n], refs[n : 2 * n]
        res_out, ffn_out = refs[2 * n :]
        gain = vec_ref[2:3, :]
        shift = vec_ref[3:4, :]
        step = rows // 2

        def body(c, carry):
            at = pl.multiple_of(c * step, 16)
            here = pl.ds(at, step)
            total = nn(mixed_refs[0][here, :], out_refs[0][...])
            for r in range(1, n):
                total = total + nn(mixed_refs[r][here, :], out_refs[r][...])
            total = total + seg_ref[here, :].astype(F32)
            res_out[here, :] = total
            xhat, _ = norm_parts(total)
            ffn_out[here, :] = (xhat * gain + shift).astype(BF16)
            return carry

        lax.fori_loop(0, 2, body, 0)

    return call(
        kernel,
        (seg, vec, *mixed, *outs),
        [((rows, width), F32), ((rows, width), BF16)],
        name="merge_attention",
        us=2.0,
        specs={2 + n + r: pl.BlockSpec((PAIR, width), lambda i: (0, 0)) for r in range(n)},
    )


def feed_forward(ffn_in, cot, wide, acc):
    rows, width = ffn_in.shape
    units = (wide.shape[0] - EXTRA - PAIR) // 2
    up_at, down_at, bias_at = PAIR, PAIR + units, PAIR + 2 * units
    n_acc = len(acc)

    def kernel(x_ref, cot_ref, ud_ref, *refs):
        acc_refs = refs[:n_acc]
        out_acc, back_acc, grad_out, act_scr, pg_scr = refs[n_acc:]
        step = rows // 2
        bias = ud_ref[bias_at : bias_at + 1, :].astype(F32)

        def body(c, total):
            at = pl.multiple_of(c * step, 16)
            here = pl.ds(at, step)
            up = ud_ref[up_at:down_at, :]
            down = ud_ref[down_at:bias_at, :]
            pre = nn(x_ref[here, :], up) + bias
            below = 0.5 + 0.5 * lax.erf(pre * 0.5**0.5)
            act = (pre * below).astype(BF16)
            slope = below + pre * (jnp.exp(-0.5 * (pre * pre)) * (1.0 / math.sqrt(2.0 * math.pi)))
            pre_grad = (nt(cot_ref[here, :], down) * slope).astype(BF16)
            act_scr[here, :] = act
            pg_scr[here, :] = pre_grad
            fwd = nn(act, down)
            back = nt(pre_grad, up)
            if n_acc:
                fwd = fwd + acc_refs[0][here, :]
                back = back + acc_refs[1][here, :]
            out_acc[here, :] = fwd
            back_acc[here, :] = back
            return total + colsum(pre_grad.astype(F32))

        total = lax.fori_loop(0, 2, body, jnp.zeros((1, units), F32))
        grad_out[0:units, :] = nn(x_ref[...].T, pg_scr[...]).astype(BF16)
        grad_out[units : 2 * units, :] = nn(act_scr[...].T, cot_ref[...]).astype(BF16)
        last = jnp.concatenate([total, jnp.zeros((EXTRA - 1, units), F32)], axis=0)
        grad_out[2 * units :, :] = last.astype(BF16)

    return call(
        kernel,
        (ffn_in, cot, wide, *acc),
        [((rows, width), F32), ((rows, width), F32), ((2 * units + EXTRA, width), BF16)],
        [pltpu.VMEM((rows, units), BF16), pltpu.VMEM((rows, units), BF16)],
        name="feed_forward",
        us=3.0,
    )


def turn_back(res, forward, backward, cot, vec, mixed_t, wides, ffn_grads, padded):
    rows, width = res.shape
    n = len(wides)
    out_rows = PAIR + EXTRA
    bias_at = ffn_grads[0].shape[0] // EXTRA - 1

    def kernel(res_ref, fwd_ref, back_ref, cot_ref, vec_ref, *refs):
        mixed_refs, out_refs, bias_refs = refs[:n], refs[n : 2 * n], refs[2 * n : 3 * n]
        block_out, resid_out, own_out, other_out, near_out = refs[3 * n : 3 * n + 5]
        dot_outs = refs[3 * n + 5 : 4 * n + 5]
        low_scr = refs[-1]
        gain = vec_ref[2:3, :]
        step = rows // 4

        def body(c, sums):
            here = pl.ds(pl.multiple_of(c * step, 16), step)
            res_rows = res_ref[here, :]
            back = back_ref[here, :]
            block_out[here, :] = (res_rows + fwd_ref[here, :]).astype(BF16)
            xhat, rstd = norm_parts(res_rows)
            resid = cot_ref[here, :].astype(F32) + norm_pull(back, gain, xhat, rstd)
            resid_out[here, :] = resid
            low_scr[here, :] = resid.astype(BF16)
            return sums[0] + colsum(back * xhat), sums[1] + colsum(back)

        zero = jnp.zeros((1, width), F32)
        gain_grad, shift_grad = lax.fori_loop(0, 4, body, (zero, zero))
        tail = jnp.zeros((EXTRA - 3, width), F32)
        low_scr[rows:, :] = jnp.zeros((padded - rows, width), BF16)
        places = [(own_out, 0), (near_out, 0), (other_out, 0), (near_out, out_rows)]
        for r, (target, at) in enumerate(places):
            dot_outs[r][...] = nt(out_refs[r][...], low_scr[...]).astype(BF16)
            grad = nn(mixed_refs[r][...], low_scr[...]).astype(BF16)
            target[at : at + PAIR, :] = grad
            last = [bias_refs[r][0:1, :].astype(F32), gain_grad, shift_grad, tail]
            target[at + PAIR : at + out_rows, :] = jnp.concatenate(last, axis=0).astype(BF16)

    return call(
        kernel,
        (res, forward, backward, cot, vec, *mixed_t, *wides, *ffn_grads),
        [((rows, width), BF16), ((rows, width), F32)]
        + [((out_rows, width), BF16)] * 2
        + [((2 * out_rows, width), BF16)]
        + [((PAIR, padded), BF16)] * n,
        [pltpu.VMEM((padded, width), BF16)],
        name="turn_back",
        us=0.5,
        specs={
            **{5 + n + r: pl.BlockSpec((PAIR, width), lambda i: (0, 0)) for r in range(n)},
            **{5 + 2 * n + r: pl.BlockSpec((EXTRA, width), lambda i: (bias_at, 0)) for r in range(n)},
        },
    )


def leave(seg, resid, acc, vec):
    rows, width = seg.shape
    padded = acc.shape[1]

    def kernel(seg_ref, resid_ref, acc_ref, vec_ref, seg_out, vec_out, acc_scr):
        gain = vec_ref[0:1, :]
        step = rows // 4
        acc_scr[...] = acc_ref[...].T

        def body(c, sums):
            here = pl.ds(pl.multiple_of(c * step, 16), step)
            grad = acc_scr[here, :]
            xhat, rstd = norm_parts(seg_ref[here, :].astype(F32))
            seg_out[here, :] = (resid_ref[here, :] + norm_pull(grad, gain, xhat, rstd)).astype(BF16)
            return sums[0] + colsum(grad * xhat), sums[1] + colsum(grad)

        zero = jnp.zeros((1, width), F32)
        gain_grad, shift_grad = lax.fori_loop(0, 4, body, (zero, zero))
        vec_out[...] = jnp.zeros(vec_out.shape, F32)
        vec_out[0:1, :] = gain_grad
        vec_out[1:2, :] = shift_grad

    return call(
        kernel,
        (seg, resid, acc, vec),
        [((rows, width), BF16), ((8, width), F32)],
        [pltpu.VMEM((padded, width), F32)],
        name="leave",
        us=0.5,
    )


def spread(mine, other, tensor_index, dtype):
    rows, width = mine.shape
    parts = [mine, swap(mine, 1), other, swap(other, 1)]

    def kernel(index_ref, *refs):
        out = refs[-1]
        for r, ref in enumerate(refs[:-1]):
            @pl.when(pl.program_id(0) == r)
            def _():
                out[0] = ref[...].astype(dtype)

    return pl.pallas_call(
        kernel,
        grid_spec=pltpu.PrefetchScalarGridSpec(
            num_scalar_prefetch=1,
            grid=(len(parts),),
            in_specs=[pl.BlockSpec((rows, width), lambda i, t: (0, 0)) for _ in parts],
            out_specs=pl.BlockSpec((1, rows, width), lambda i, t: (t[0] ^ i, 0, 0)),
        ),
        out_shape=jax.ShapeDtypeStruct((len(parts), rows, width), dtype),
        compiler_params=pltpu.CompilerParams(vmem_limit_bytes=24 * 1024 * 1024),
        cost_estimate=pl.CostEstimate(flops=1000, bytes_accessed=1000, transcendentals=0),
        name="spread",
    )(jnp.reshape(tensor_index, (1,)).astype(jnp.int32), *parts)


def own_shares(norm_vecs, ffn_vecs, place, share):
    width = ffn_vecs.shape[1]

    def kernel(place_ref, norm_ref, ffn_ref, *outs):
        whole = jnp.concatenate([norm_ref[3:5, :], ffn_ref[0:3, :]], axis=0)
        total = jnp.zeros((whole.shape[0], share), F32)
        for k in range(width // share):
            part = whole[:, k * share : (k + 1) * share]
            total = total + jnp.where(place_ref[0] == k, part, jnp.zeros_like(part))
        for v, out in enumerate(outs):
            out[...] = total[v : v + 1]

    outs = call(
        kernel,
        (jnp.reshape(place, (1,)).astype(jnp.int32), norm_vecs, ffn_vecs),
        [((1, share), F32)] * 5,
        scalars=1,
        name="own_shares",
    )
    return [o.reshape(share) for o in outs]


def rotary_tables(starts, padded):
    half = HEAD // 2
    inverse = jnp.exp(jnp.arange(half).astype(F32) * (-math.log(10000.0) / half))
    angles = inverse[:, None] * starts.astype(F32)[None, :]
    angles = jnp.pad(angles, ((0, 0), (0, padded - starts.shape[0])))
    return jnp.cos(angles), jnp.sin(angles)


def vector_rows(vectors, here, width, cols):
    own = vectors[0].shape[0]
    stacked = jnp.stack(vectors + (jnp.zeros_like(vectors[0]),) * (8 - len(vectors)))
    lanes = -(-cols // own) * own

    def kernel(here_ref, vec_ref, out):
        tiled = jnp.concatenate([vec_ref[...].astype(F32)] * (lanes // own), axis=1)[:, 0:cols]
        place = lax.broadcasted_iota(jnp.int32, tiled.shape, 1)
        first = here_ref[0] * own
        rows = []
        for v in range(len(vectors)):
            for at in (0, cols):
                inside = (place + at >= first) & (place + at < first + own)
                rows.append(jnp.where(inside, tiled, 0.0)[v : v + 1])
        rows.append(jnp.zeros((EXTRA - len(rows), cols), F32))
        out[...] = jnp.concatenate(rows, axis=0).astype(BF16)

    return call(
        kernel,
        (jnp.reshape(here, (1,)).astype(jnp.int32), stacked),
        [((EXTRA, cols), BF16)],
        scalars=1,
        name="vector_rows",
        us=0.3,
    )[0]


def local(
    segments,
    seg_start,
    seg_count,
    norm_gain,
    norm_shift,
    qkv_weight,
    out_weight,
    ffn_gain,
    ffn_shift,
    up_weight,
    up_bias,
    down_weight,
    cotangent,
):
    seq_local, seg_len, width = segments.shape
    tensor = lax.axis_size("tensor")
    members = lax.axis_size("dp")
    assert seq_local == tensor == 4
    padded = -(-seg_len // BLOCK) * BLOCK
    bits = bits_of(members)
    here = lax.axis_index("dp")
    mine = lax.axis_index("tensor")
    cols = 3 * qkv_weight.shape[2]
    assert cols == 3 * PAIR and width * 2 > cols
    groups = range(tensor)
    thin = any(
        a.shape[0] % 16 for a in (qkv_weight, out_weight, up_weight, down_weight)
    )

    seg = lax.dynamic_index_in_dim(segments, mine, 0, keepdims=False)
    cot = lax.dynamic_index_in_dim(cotangent, mine, 0, keepdims=False)
    starts = lax.dynamic_index_in_dim(seg_start, mine, 0, keepdims=False)
    live = lax.dynamic_slice_in_dim(seg_count, mine, 1)
    cos, sin = rotary_tables(starts, padded)

    def indices(distances):
        return here ^ jnp.asarray(distances, jnp.int32)

    qkv_rows, out_rows = qkv_weight.shape[0], out_weight.shape[0]
    up_rows, down_rows = up_weight.shape[0], down_weight.shape[0]
    vectors = (norm_gain, norm_shift, ffn_gain, ffn_shift, up_bias)
    first = jnp.concatenate(
        [qkv_weight.reshape(-1, cols), vector_rows(vectors, here, width, cols)]
    )
    arrays, order = [first[None]], [0]
    side, side_order = [jnp.concatenate([out_weight, up_weight])[None]], [0]
    down, down_order = [down_weight[None]], [0]
    for bit in bits[:-1]:
        arrays, order = widened(arrays, order, bit)
        side, side_order = widened(side, side_order, bit)
        down, down_order = widened(down, down_order, bit)
    arrays, order = widened(arrays, order, bits[-1])
    side, side_order = widened(side, side_order, bits[-1])
    down = joined(down)
    down = [down, swap(down, 2)]
    down_far = [across(d, bits[-1]) for d in down]
    down_order = down_order + [o ^ bits[-1] for o in down_order]

    pieces, places, parts = in_place(arrays, indices(order), (qkv_rows,))
    w0, xt, vec = enter(seg, pieces, places, parts[0], seg_len, padded, width, cols)
    def weights_of(side, down, w):
        s, s_places, s_parts = in_place(side, indices(side_order), (out_rows, up_rows))
        d, d_places, d_parts = in_place(down, indices(down_order), (down_rows,))
        return lay_out(s, d, (s_places, d_places), (s_parts, d_parts), w, width)

    def attend(w):
        return list(attend_forward(live, xt, w, cos, sin, seg_len))

    w = [w0, swap(w0, 1), swap(w0, 2), None]
    far = [swap(s, 2) for s in side]
    heads = [attend(w[0])]
    w[1], heads[0][2] = gate(w[1], heads[0][2])
    heads.append(attend(w[1]))
    *near, heads[1][2] = gate(*side, down[0], down_far[0], heads[1][2])
    wides = [weights_of(near[:-2], near[-2:], w0)]
    wides.append(swap(wides[0], 1))
    w[2], wides[0] = gate(w[2], wides[0])
    w[3] = swap(w[2], 1)
    heads.append(attend(w[2]))
    w[3], heads[2][2] = gate(w[3], heads[2][2])
    heads.append(attend(w[3]))
    *far, heads[3][2] = gate(*far, down[1], down_far[1], heads[3][2])
    wides.append(weights_of(far[:-2], far[-2:], w[2]))
    wides.append(swap(wides[2], 1))
    res, ffn_in = merge_attention(seg, [h[2] for h in heads], wides, vec)
    up_bits, down_bits = bits[::-1], bits[-2::-1] + bits[-1:]
    ahead, down_ahead = (indices(halving_order(b)) for b in (up_bits, down_bits))
    acc = ()
    ffn_grads = [None] * 4
    for r in (3, 2, 1, 0):
        out_acc, back_acc, ffn_grads[r] = feed_forward(ffn_in, cot, wides[r], acc)
        acc = (out_acc, back_acc)
    ups = (ffn_grads[0], swap(ffn_grads[1], 1), ffn_grads[2], swap(ffn_grads[3], 1))
    units = (ffn_grads[0].shape[0] - EXTRA) // 2
    if thin:
        pairs = [added(ups[0:2]), added(ups[2:4])]
        keep = lambda rows: rows
        up_halves = cut_thin([[p[:units]] for p in pairs], ahead, [(0, up_rows, keep)])
        down_halves = cut_thin(
            [[p[units : 2 * units]] for p in pairs], down_ahead, [(0, down_rows, keep)]
        )
    else:
        up_halves, down_halves = cut_ffn(ups, ahead, down_ahead, up_rows)
    res, up_halves, down_halves = lax.optimization_barrier((res, up_halves, down_halves))
    up = Halving(up_halves, [(across, b) for b in up_bits])
    down = Halving(down_halves, [(across, b) for b in down_bits])
    turned = turn_back(
        res, *acc, cot, vec, [h[1] for h in heads], wides, ffn_grads, padded
    )
    block_mine, resid, out_own, out_other, out_near = turned[0:5]
    dots = list(turned[5:9])
    block_out = spread(block_mine, swap(block_mine, 2), mine, BF16)
    out_near = swap(out_near, 1)
    out_far = swap(added([out_other, out_near[out_other.shape[0] :]]), 2)

    acc = ()
    qkv_grads = [None] * 4
    for r in (3, 2, 1, 0):
        if r == 2:
            up.step()
            down.step()
            dots[r], up.kept, up.sent, down.kept, down.sent = gate(
                dots[r], up.kept, up.sent, down.kept, down.sent
            )
        if r == 1:
            dots[r], other, out_far = gate(dots[r], other, out_far)
        qkv, ot, _, lse = heads[r]
        total, qkv_grads[r] = attend_backward(
            live, xt, w[r], cos, sin, qkv, ot, lse, dots[r], acc, seg_len
        )
        acc = (total,)
        if r == 2:
            other = added([qkv_grads[2], swap(qkv_grads[3], 1)])
    up.step()
    down.step()
    total, up.kept, up.sent, down.kept, down.sent = gate(
        total, up.kept, up.sent, down.kept, down.sent
    )
    seg_mine, norm_vec = leave(seg, resid, total, vec)
    seg_mine = Held(seg_mine)
    seg_other = Held(swap(seg_mine.kept, 2))
    other, seg_mine.kept = gate(swap(other, 2), seg_mine.kept)
    parts = (qkv_grads[0], swap(qkv_grads[1], 1), other)
    if thin:
        tall = out_own.shape[0]
        out_sum = added([out_own, out_near[:tall], out_far])
        last = out_sum[-EXTRA:].at[3:5].set(norm_vec[0:2].astype(BF16))
        halves = cut_thin(
            [[added(parts), out_sum]], ahead, [(0, qkv_rows, packed), (1, out_rows, keep)], [last]
        )
    else:
        halves = cut_heads(parts, norm_vec, (out_own, out_near, out_far), ahead, qkv_rows, out_rows)
    heads_sum = Halving(halves, [(across, b) for b in up_bits])
    down.step(heads_sum)
    block_out, down.kept = gate(block_out, down.kept)
    up.step(down)
    heads_sum.step(up)
    both = swap(jnp.concatenate([up.sent, down.sent]), 2)
    while len(heads_sum.steps) > 1:
        heads_sum.step()
    seg_other.kept, heads_sum.kept, heads_sum.sent = gate(
        seg_other.kept, heads_sum.kept, heads_sum.sent
    )
    got = across(heads_sum.sent, heads_sum.steps[0][1])
    segments_grad = spread(seg_mine.kept, seg_other.kept, mine, F32)
    got, segments_grad = gate(got, segments_grad)
    up_g, down_g = end_ffn(up.kept, down.kept, both)
    if thin:
        total = heads_sum.kept[0].astype(F32) + got[0].astype(F32)
        high = 3 * qkv_rows // 4
        qkv_g = unpacked(total[:high])
        out_g, vecs = total[high : high + out_rows], total[high + out_rows :]
    else:
        qkv_g, out_g, vecs = end_heads(heads_sum.kept, got, qkv_rows, out_rows)
    near_vecs = vecs + swap(vecs, 1)
    far_vecs, up_g, down_g = gate(swap(near_vecs, 2), up_g, down_g)
    norm_vecs = near_vecs + far_vecs

    share = norm_gain.shape[0]
    assert cols % share == 0
    assert up_bias.shape[0] == share
    norm_gain_g, norm_shift_g, bias_g, ffn_gain_g, ffn_shift_g = own_shares(
        norm_vecs, vecs, here, share
    )
    return (
        block_out,
        segments_grad,
        norm_gain_g,
        norm_shift_g,
        qkv_g,
        out_g,
        ffn_gain_g,
        ffn_shift_g,
        up_g,
        bias_g,
        down_g,
    )


def solution(mesh):
    placed = (
        P("dp", None, None),
        P("dp", None),
        P("dp"),
        P("dp"),
        P("dp"),
        P("dp", None, "tensor"),
        P(("tensor", "dp"), None),
        P("dp"),
        P("dp"),
        P("dp", "tensor"),
        P(("tensor", "dp")),
        P(("tensor", "dp"), None),
        P("dp", None, None),
    )
    return jax.shard_map(
        local,
        mesh=mesh,
        in_specs=placed,
        out_specs=(
            P("dp", None, None),
            P("dp", None, None),
            P("dp"),
            P("dp"),
            P("dp", None, "tensor"),
            P(("tensor", "dp"), None),
            P("dp"),
            P("dp"),
            P("dp", "tensor"),
            P(("tensor", "dp")),
            P(("tensor", "dp"), None),
        ),
        check_vma=False,
    )
```
